256 devices in a mesh: layer: 2 (over z_lo), row: 8 (over y, core), col: 16 (over z_hi, x).
Axes of the slice: x: 4, y: 4, z: 8 (z_hi: 4, z_lo: 2; z = z_hi * 2 + z_lo), core: 2. Of those that a mesh axis runs over, the one named last changes fastest.
Arguments:
- matrix: float32 [16384, 16384], P('row', 'col'), may hold values from -1.5 to 1.5, as said below
Outputs:
- square_panel: float32 [16384, 512], P('row', 'layer')
- new_panel: float32 [16384, 512], P('row', 'layer')
The draws below stay inside these ranges and needn't reach their ends.
Inputs may be any that keep to these rules, and one draw needn't show every extreme that they name: `matrix`: entries off the diagonal are of order 0.5 / sqrt(16384); the diagonal's magnitudes lie between 0.6 and 1 with either sign.
All inputs are finite; a program needn't handle non-finite values.
Results may differ from the reference program's by a relative error of at most 0.000076.
Values sent between devices are 32-bit elements; how exact they have to be, the bound alone decides.
A program may use at most 128 MiB of HBM per device.

```python
import jax
import jax.numpy as jnp
from jax import lax

N = 16384
PW = 512


def draw_matrix(key, part):
    key_off = jax.random.fold_in(key, 11)
    key_mag = jax.random.fold_in(key, 12)
    key_sign = jax.random.fold_in(key, 13)
    entries = jax.random.normal(key_off, (N, N), jnp.float32)
    entries = entries * (0.5 / jnp.sqrt(jnp.float32(N)))
    magnitude = jax.random.uniform(key_mag, (N,), jnp.float32, 0.6, 1.0)
    signs = (2 * jax.random.randint(key_sign, (N,), 0, 2) - 1).astype(jnp.float32)
    diagonal_index = jnp.arange(N)
    entries = entries.at[diagonal_index, diagonal_index].add(magnitude * signs)
    return entries


def setup_inputs(seed: int = 0) -> dict:
    keys = jax.random.split(jax.random.key(seed), 2)
    matrix = draw_matrix(jax.random.fold_in(keys[1], 71), 0)
    return dict(matrix=matrix)


def matmul_high(left_side, right_side):
    return jnp.dot(left_side, right_side, precision=lax.Precision.HIGHEST, preferred_element_type=jnp.float32)


def reference(matrix):
    panel_block = matrix[:, :PW]
    square_panel = matmul_high(matrix, panel_block)
    update = matmul_high(matrix, square_panel)
    new_panel = (3.0 * panel_block - update) * 0.5
    return square_panel, new_panel
```

```python
import functools

import jax
import jax.numpy as jnp
from jax import lax
from jax.experimental import pallas as pl
from jax.experimental.pallas import tpu as pltpu
from jax.sharding import PartitionSpec as P

MESH = pl.DeviceIdType.MESH
F32 = jnp.float32
BF16 = jnp.bfloat16

CHUNKS = 2
W = 128
LAG = 2
ROWS = 2048
DEPTH = 1024
SLICE = 512
SUB = 128
TILE = 256
NSEM = 160


class Sems:
    def __init__(self, send, recv):
        self.send, self.recv, self.n, self.pending = send, recv, 0, []

    def new(self):
        self.n += 1
        assert self.n <= NSEM
        return self.n - 1

    def copy(self, src, dst, slot, device):
        return pltpu.make_async_remote_copy(
            src_ref=src,
            dst_ref=dst,
            send_sem=self.send.at[slot],
            recv_sem=self.recv.at[slot],
            device_id=device,
            device_id_type=MESH,
        )


def kernel(
    x_hbm, s_hbm, n_hbm,
    xf, xh, xl, pb, pc, sc, hl, part, rx1, rx2, rz1, rz2, full,
    send_sem, recv_sem, load_sem, panel_sem, out_sem,
):
    layer = lax.axis_index("layer")
    row = lax.axis_index("row")
    col = lax.axis_index("col")
    y, q = lax.div(row, 2), lax.rem(row, 2)
    zh, x = lax.div(col, 4), lax.rem(col, 4)
    owner_core = lax.div(x, 2)
    half = lax.rem(x, 2)
    sems = Sems(send_sem, recv_sem)
    drains = []

    def m8(value, n):
        return pl.ds(pl.multiple_of(value, 64), n)

    def at_x(d):
        return {"col": zh * 4 + lax.rem(x + d, 4)}

    def at_z(d):
        return {"col": lax.rem(zh + d, 4) * 4 + x}

    def at_y(d):
        return {"row": lax.rem(y + d, 4) * 2 + q}

    partner = {"row": y * 2 + 1 - q}
    fetches = q == owner_core
    has_panel = col == 0
    origin = jnp.logical_and(jnp.logical_and(y == 0, q == 0), has_panel)

    loads = [
        pltpu.make_async_copy(
            x_hbm.at[pl.ds(i * TILE, TILE), :], xf.at[pl.ds(i * TILE, TILE), :], load_sem.at[i]
        )
        for i in range(ROWS // TILE)
    ]
    panel_loads = [
        pltpu.make_async_copy(
            x_hbm.at[:, pl.ds(pl.multiple_of(layer * (CHUNKS * W) + k * W, W), W)],
            pb.at[k],
            panel_sem.at[k],
        )
        for k in range(CHUNKS)
    ]

    @pl.when(has_panel)
    def _():
        for load in panel_loads:
            load.start()

    for load in loads:
        load.start()

    barrier = pltpu.get_barrier_semaphore()
    for device in (at_x(1), at_x(3), at_z(1), at_z(3), at_y(1), at_y(2), at_y(3), partner):
        pl.semaphore_signal(barrier, inc=1, device_id=device, device_id_type=MESH)

    @pl.when(jnp.logical_and(fetches, jnp.logical_not(origin)))
    def _():
        pl.semaphore_signal(
            barrier, inc=1, device_id={"row": zh * 2 + q, "col": 0}, device_id_type=MESH
        )

    @pl.when(has_panel)
    def _():
        pl.semaphore_wait(barrier, 16 - jnp.where(row == 0, 1, 0))

    @pl.when(jnp.logical_not(has_panel))
    def _():
        pl.semaphore_wait(barrier, 8)

    def owned(d):
        u = lax.rem(x + d - 2 * q + 4, 4)
        return (2 * lax.rem(lax.div(u + 1, 2), 2) + lax.div(u, 2)) * SLICE

    x_rows = [owned(d) for d in range(4)]

    def z_rows(d):
        return x_rows[0] + lax.rem(zh + d, 4) * SUB

    def reduce_start(buf, r1, rows, size, at):
        h = size // 2
        a = sems.copy(buf.at[m8(rows[2], h)], r1.at[0], sems.new(), at(1))
        b = sems.copy(buf.at[m8(rows[2] + h, h)], r1.at[1], sems.new(), at(3))
        a.start()
        b.start()
        drains.extend([a, b])
        return a, b

    def reduce_own(buf, r2, rows, size, at):
        h = size // 2
        a = sems.copy(buf.at[m8(rows[1] + h, h)], r2.at[0, pl.ds(h, h)], sems.new(), at(1))
        b = sems.copy(buf.at[m8(rows[3], h)], r2.at[1, pl.ds(0, h)], sems.new(), at(3))
        a.start()
        b.start()
        drains.extend([a, b])
        return a, b

    def reduce_middle(buf, r1, r2, rows, size, at, first):
        h = size // 2
        first[0].wait_recv()
        buf[m8(rows[1], h)] += r1[0]
        a = sems.copy(buf.at[m8(rows[1], h)], r2.at[0, pl.ds(0, h)], sems.new(), at(1))
        a.start()
        first[1].wait_recv()
        buf[m8(rows[3] + h, h)] += r1[1]
        b = sems.copy(buf.at[m8(rows[3] + h, h)], r2.at[1, pl.ds(h, h)], sems.new(), at(3))
        b.start()
        drains.extend([a, b])
        return a, b

    def gather_start(buf, rows, size, at):
        a = sems.copy(buf.at[m8(rows[0], size)], buf.at[m8(rows[0], size)], sems.new(), at(1))
        b = sems.copy(buf.at[m8(rows[0], size)], buf.at[m8(rows[0], size)], sems.new(), at(3))
        a.start()
        b.start()
        drains.extend([a, b])
        return a, b

    def gather_middle(buf, rows, size, at, first):
        h = size // 2
        first[0].wait_recv()
        a = sems.copy(buf.at[m8(rows[3], h)], buf.at[m8(rows[3], h)], sems.new(), at(1))
        a.start()
        first[1].wait_recv()
        b = sems.copy(buf.at[m8(rows[1] + h, h)], buf.at[m8(rows[1] + h, h)], sems.new(), at(3))
        b.start()
        drains.extend([a, b])
        return a, b

    def split_rhs(src, k):
        def tile(i, carry):
            rows = pl.ds(pl.multiple_of(i * TILE, TILE), TILE)
            value = src[rows, :]
            hi = value.astype(BF16)
            hl[k, rows, pl.ds(0, W)] = hi
            hl[k, rows, pl.ds(W, W)] = (value - hi.astype(F32)).astype(BF16)
            return carry

        lax.fori_loop(0, DEPTH // TILE, tile, 0)

    def product(buf, k, first_row):
        def tile(i, carry):
            rows = pl.ds(pl.multiple_of(first_row + i * TILE, TILE), TILE)
            both = jnp.dot(xh[rows, :], hl[k], preferred_element_type=F32)
            low = jnp.dot(xl[rows, :], hl[k, :, pl.ds(0, W)], preferred_element_type=F32)
            buf[rows, :] = both[:, :W] + (both[:, W:] + low)
            return carry

        lax.fori_loop(0, SLICE // TILE, tile, 0)

    def minus_panel(buf, k, first_row):
        @pl.when(has_panel)
        def _():
            rows = m8(first_row, SLICE)
            buf[rows, :] -= 3.0 * pb[k, rows, :]

    def split_block():
        for i, load in enumerate(loads):
            load.wait()

        def tile(i, carry):
            rows = pl.ds(pl.multiple_of(i * 64, 64), 64)
            value = xf[rows, :]
            hi = value.astype(BF16)
            xh[rows, :] = hi
            xl[rows, :] = (value - hi.astype(F32)).astype(BF16)
            return carry

        lax.fori_loop(0, ROWS // 64, tile, 0)

    def chain(k):
        steps = []
        state = {}

        quarter = DEPTH // 4
        spread = [sems.new() for _ in range(1)]
        sent_panel = []

        def panel_send():
            @pl.when(has_panel)
            def _():
                panel_loads[k].wait()

            for h in range(2):
                for j in range(4):
                    slot = sems.new()
                    src = pb.at[k, pl.ds(h * DEPTH + j * quarter, quarter)]
                    dst = pc.at[k, pl.ds(j * quarter, quarter)]
                    copy = pltpu.make_async_remote_copy(
                        src_ref=src,
                        dst_ref=dst,
                        send_sem=send_sem.at[slot],
                        recv_sem=recv_sem.at[spread[0]],
                        device_id={"row": 2 * j + q, "col": y * 4 + 2 * q + h},
                        device_id_type=MESH,
                    )
                    if h == 0 and j == 0:

                        @pl.when(origin)
                        def _():
                            pc[k, pl.ds(0, quarter)] = pb[k, pl.ds(0, quarter)]

                        @pl.when(jnp.logical_and(has_panel, row != 0))
                        def _(copy=copy):
                            copy.start()
                    else:

                        @pl.when(has_panel)
                        def _(copy=copy):
                            copy.start()

                    sent_panel.append(copy)

            state["panel_sent"] = sent_panel

        ring = [sems.new() for _ in range(4)]
        share = [sems.new() for _ in range(4)]

        def mine(d):
            return m8(lax.rem(y + 4 - d, 4) * quarter, quarter)

        def ring_copy(d):
            return sems.copy(pc.at[k, mine(0)], pc.at[k, mine(0)], ring[d], at_y(d))

        def share_copy(d):
            return sems.copy(pc.at[k, mine(d)], pc.at[k, mine(d)], share[d], partner)

        def panel_ring():
            @pl.when(fetches)
            def _():
                @pl.when(jnp.logical_not(origin))
                def _():
                    pltpu.make_async_remote_copy(
                        src_ref=pc.at[k, mine(0)],
                        dst_ref=pc.at[k, mine(0)],
                        send_sem=send_sem.at[spread[0]],
                        recv_sem=recv_sem.at[spread[0]],
                        device_id=partner,
                        device_id_type=MESH,
                    ).wait_recv()

                for d in (1, 3, 2):
                    ring_copy(d).start()
                share_copy(0).start()

        def panel_share():
            @pl.when(fetches)
            def _():
                for d in (1, 3, 2):
                    ring_copy(d).wait_recv()
                    share_copy(d).start()

            @pl.when(jnp.logical_not(fetches))
            def _():
                for d in range(4):
                    share_copy(d).wait_recv()

        def panel_drain():
            for i, copy in enumerate(sent_panel):
                cond = jnp.logical_and(has_panel, row != 0) if i == 0 else has_panel

                @pl.when(cond)
                def _(copy=copy):
                    copy.wait_send()

            @pl.when(fetches)
            def _():
                for d in range(4):
                    if d:
                        ring_copy(d).wait_send()
                    share_copy(d).wait_send()

        def multiply(phase):
            buf = part.at[phase, k]

            def run(first_row):
                product(buf, k, first_row)
                if phase == 1:
                    minus_panel(buf, k, first_row)

            def step():
                if phase == 0 and k == 0:
                    split_block()
                split_rhs((pc if phase == 0 else sc).at[k], k)
                run(x_rows[2])
                state[phase, "x1"] = reduce_start(buf, rx1.at[phase, k], x_rows, SLICE, at_x)
                run(x_rows[1])
                run(x_rows[3])
                state[phase, "x2"] = reduce_own(buf, rx2.at[phase, k], x_rows, SLICE, at_x)
                run(x_rows[0])

            return step

        def reduce_steps(phase):
            buf = part.at[phase, k]
            out = full.at[phase, k]
            zr = [z_rows(d) for d in range(4)]

            def x_middle():
                state[phase, "x3"] = reduce_middle(
                    buf, rx1.at[phase, k], rx2.at[phase, k], x_rows, SLICE, at_x, state[phase, "x1"]
                )

            def x_end():
                for copy in state[phase, "x2"] + state[phase, "x3"]:
                    copy.wait_recv()
                rows = m8(x_rows[0], SLICE)
                buf[rows] += rx2[phase, k, 0] + rx2[phase, k, 1]
                state[phase, "z1"] = reduce_start(buf, rz1.at[phase, k], zr, SUB, at_z)
                state[phase, "z2"] = reduce_own(buf, rz2.at[phase, k], zr, SUB, at_z)

            def z_middle():
                state[phase, "z3"] = reduce_middle(
                    buf, rz1.at[phase, k], rz2.at[phase, k], zr, SUB, at_z, state[phase, "z1"]
                )

            def z_end():
                for copy in state[phase, "z2"] + state[phase, "z3"]:
                    copy.wait_recv()
                rows = m8(zr[0], SUB)
                total = buf[rows] + (rz2[phase, k, 0] + rz2[phase, k, 1])
                out[rows] = total if phase == 0 else total * -0.5
                state[phase, "g1"] = gather_start(out, zr, SUB, at_z)

            def gz_middle():
                state[phase, "g2"] = gather_middle(out, zr, SUB, at_z, state[phase, "g1"])

            return [x_middle, x_end, z_middle, z_end, gz_middle]

        def gather_x(phase):
            out = full.at[phase, k]

            def start():
                for copy in state[phase, "g2"]:
                    copy.wait_recv()
                state[phase, "g3"] = gather_start(out, x_rows, SLICE, at_x)

            def middle():
                state[phase, "g4"] = gather_middle(out, x_rows, SLICE, at_x, state[phase, "g3"])

            def end():
                for copy in state[phase, "g4"]:
                    copy.wait_recv()
                store = pltpu.make_async_copy(
                    out,
                    (s_hbm if phase == 0 else n_hbm).at[:, pl.ds(k * W, W)],
                    out_sem.at[phase, k],
                )
                store.start()
                state[phase, "store"] = store

            return start, middle, end

        turn = lax.rem(y - zh + 4, 4)
        root = jnp.logical_and(fetches, turn == 0)
        y1 = jnp.logical_and(fetches, turn == 1)
        y2 = jnp.logical_and(fetches, turn == 2)
        y3 = jnp.logical_and(fetches, turn == 3)
        slab = [m8(half * DEPTH + i * SLICE, SLICE) for i in range(2)]
        fwd = [[sems.new() for _ in range(2)] for _ in range(4)]

        def from_root(i, d):
            return sems.copy(full.at[0, k, slab[i]], sc.at[k, pl.ds(i * SLICE, SLICE)], fwd[d][i], at_y(d))

        def onward(i, d):
            block = sc.at[k, pl.ds(i * SLICE, SLICE)]
            return sems.copy(block, block, fwd[2][i], at_y(d))

        def across(i):
            block = sc.at[k, pl.ds(i * SLICE, SLICE)]
            return sems.copy(block, block, fwd[0][i], partner)

        def send_slab(i):
            @pl.when(root)
            def _():
                from_root(i, 1).start()
                from_root(i, 3).start()
                sc[k, pl.ds(i * SLICE, SLICE)] = full[0, k, slab[i]]
                across(i).start()

        def pass_slab():
            @pl.when(y1)
            def _():
                from_root(0, 1).wait_recv()
                onward(0, 1).start()
                across(0).start()
                from_root(1, 1).wait_recv()
                across(1).start()

            @pl.when(y3)
            def _():
                from_root(0, 3).wait_recv()
                across(0).start()
                from_root(1, 3).wait_recv()
                onward(1, 3).start()
                across(1).start()

        def end_slab():
            @pl.when(y2)
            def _():
                onward(0, 1).wait_recv()
                across(0).start()
                onward(1, 3).wait_recv()
                across(1).start()

            @pl.when(jnp.logical_not(fetches))
            def _():
                across(0).wait_recv()
                across(1).wait_recv()

        def slab_drain():
            @pl.when(root)
            def _():
                for i in range(2):
                    from_root(i, 1).wait_send()
                    from_root(i, 3).wait_send()

            @pl.when(y1)
            def _():
                onward(0, 1).wait_send()

            @pl.when(y3)
            def _():
                onward(1, 3).wait_send()

            @pl.when(fetches)
            def _():
                across(0).wait_send()
                across(1).wait_send()

        s_start, s_middle, s_end = gather_x(0)
        u_start, u_middle, u_end = gather_x(1)

        def s_start_and_slab():
            s_start()
            send_slab(0)

        def s_middle_and_slab():
            s_middle()
            send_slab(1)

        def pass_on():
            pass_slab()

        def multiply_again():
            end_slab()
            multiply(1)()

        second = reduce_steps(1)

        def finish():
            s_end()

        steps += [panel_send, panel_ring, panel_share, multiply(0)]
        steps += reduce_steps(0)
        steps += [s_start_and_slab, s_middle_and_slab, pass_on, multiply_again]
        steps += [second[0], finish] + second[1:]
        steps += [u_start, u_middle, u_end]
        return steps, [panel_drain, slab_drain], state

    chains = [chain(k) for k in range(CHUNKS)]
    for t in range(len(chains[0][0]) + LAG * (CHUNKS - 1)):
        for k in range(CHUNKS):
            if 0 <= t - LAG * k < len(chains[k][0]):
                chains[k][0][t - LAG * k]()
    for copy in drains:
        copy.wait_send()
    for steps, ends, state in chains:
        for end in ends:
            end()
        for phase in range(2):
            state[phase, "store"].wait()


def solution(mesh):
    def body(matrix):
        return pl.pallas_call(
            kernel,
            out_shape=(
                jax.ShapeDtypeStruct((ROWS, CHUNKS * W), F32),
                jax.ShapeDtypeStruct((ROWS, CHUNKS * W), F32),
            ),
            in_specs=[pl.BlockSpec(memory_space=pl.ANY)],
            out_specs=(pl.BlockSpec(memory_space=pl.ANY), pl.BlockSpec(memory_space=pl.ANY)),
            scratch_shapes=[
                pltpu.VMEM((ROWS, DEPTH), F32),
                pltpu.VMEM((ROWS, DEPTH), BF16),
                pltpu.VMEM((ROWS, DEPTH), BF16),
                pltpu.VMEM((CHUNKS, ROWS, W), F32),
                pltpu.VMEM((CHUNKS, DEPTH, W), F32),
                pltpu.VMEM((CHUNKS, DEPTH, W), F32),
                pltpu.VMEM((CHUNKS, DEPTH, 2 * W), BF16),
                pltpu.VMEM((2, CHUNKS, ROWS, W), F32),
                pltpu.VMEM((2, CHUNKS, 2, SLICE // 2, W), F32),
                pltpu.VMEM((2, CHUNKS, 2, SLICE, W), F32),
                pltpu.VMEM((2, CHUNKS, 2, SUB // 2, W), F32),
                pltpu.VMEM((2, CHUNKS, 2, SUB, W), F32),
                pltpu.VMEM((2, CHUNKS, ROWS, W), F32),
                pltpu.SemaphoreType.DMA((NSEM,)),
                pltpu.SemaphoreType.DMA((NSEM,)),
                pltpu.SemaphoreType.DMA((ROWS // TILE,)),
                pltpu.SemaphoreType.DMA((CHUNKS,)),
                pltpu.SemaphoreType.DMA((2, CHUNKS)),
            ],
            compiler_params=pltpu.CompilerParams(
                collective_id=0, has_side_effects=True, vmem_limit_bytes=60 * 1024 * 1024
            ),
        )(matrix)

    return jax.shard_map(
        body,
        mesh=mesh,
        in_specs=(P("row", "col"),),
        out_specs=(P("row", "layer"), P("row", "layer")),
        check_vma=False,
    )
```

```python
import functools

import jax
import jax.numpy as jnp
from jax import lax
from jax.experimental import pallas as pl
from jax.experimental.pallas import tpu as pltpu
from jax.sharding import PartitionSpec as P

MESH = pl.DeviceIdType.MESH
F32 = jnp.float32
BF16 = jnp.bfloat16

CHUNKS = 2
W = 128
ROWS = 2048
DEPTH = 1024
SLICE = 512
SUB = 128
TILE = 512
QUARTER = 256
STEP = 256
NRECV = CHUNKS * (15 + 18 * 2)
NSEND = CHUNKS * 15
UNITS = 2
US = 512 // UNITS
UZ = 128 // UNITS


ORDER = (
    (0, "p", 0), (1, "p", 0), "split", (0, "p", 1), (0, "p", 2), (1, "p", 1), (1, "p", 2), (0, "p", 3), (0, "p", 4),
    (0, "m", 0), (1, "p", 3), (0, "u", 0, 0, 0), (0, "u", 0, 1, 0), (1, "p", 4), (0, "u", 0, 0, 1), (1, "m", 0),
    (0, "u", 0, 1, 1), (0, "u", 0, 0, 2), (1, "u", 0, 0, 0), (1, "u", 0, 1, 0), (0, "u", 0, 1, 2), (0, "u", 0, 0, 3),
    (1, "u", 0, 0, 1), (0, "u", 0, 1, 3), (1, "u", 0, 1, 1), (0, "u", 0, 0, 4), (1, "u", 0, 0, 2), (0, "u", 0, 1, 4),
    (1, "u", 0, 1, 2), (0, "u", 0, 0, 5), (1, "u", 0, 0, 3), (0, "u", 0, 1, 5), (1, "u", 0, 1, 3), (0, "s", 0, 0),
    (0, "u", 0, 0, 6), (0, "s", 1, 0), (1, "u", 0, 0, 4), (1, "u", 0, 1, 4), (0, "e", 0, 0), (0, "u", 0, 1, 6),
    (0, "s", 0, 1), (0, "e", 1, 0), (1, "u", 0, 0, 5), (0, "u", 0, 0, 7), (1, "u", 0, 1, 5), (0, "s", 1, 1),
    (0, "u", 0, 1, 7), (0, "e", 0, 1), (1, "s", 0, 0), (1, "u", 0, 0, 6), (1, "s", 1, 0), (0, "e", 1, 1), (0, "m", 1),
    (1, "e", 0, 0), (1, "u", 0, 1, 6), (1, "s", 0, 1), (1, "e", 1, 0), (1, "u", 0, 0, 7), (0, "u", 1, 0, 0),
    (0, "u", 1, 1, 0), (1, "s", 1, 1), (1, "e", 0, 1), (1, "u", 0, 1, 7), (1, "e", 1, 1), (0, "u", 1, 0, 1),
    (1, "m", 1), (0, "u", 1, 1, 1), (0, "u", 1, 0, 2), (1, "u", 1, 0, 0), (1, "u", 1, 1, 0), (0, "u", 1, 1, 2),
    (0, "u", 1, 0, 3), (1, "u", 1, 0, 1), (0, "u", 1, 1, 3), (1, "u", 1, 1, 1), (0, "u", 1, 0, 4), (1, "u", 1, 0, 2),
    (0, "u", 1, 1, 4), (1, "u", 1, 1, 2), (0, "u", 1, 0, 5), (1, "u", 1, 0, 3), (0, "u", 1, 1, 5), (1, "u", 1, 1, 3),
    (0, "u", 1, 0, 6), (1, "u", 1, 0, 4), (1, "u", 1, 1, 4), (0, "u", 1, 1, 6), (1, "u", 1, 0, 5), (0, "u", 1, 0, 7),
    (1, "u", 1, 1, 5), (0, "u", 1, 1, 7), (1, "u", 1, 0, 6), (1, "u", 1, 1, 6), (1, "u", 1, 0, 7), (1, "u", 1, 1, 7),
)


class Sems:
    def __init__(self, send, recv, anyone):
        self.send, self.recv, self.anyone, self.n_send, self.n_recv = send, recv, anyone, 0, 0

    def new_send(self):
        self.n_send += 1
        assert self.n_send <= NSEND
        return self.n_send - 1

    def new_recv(self):
        self.n_recv += 1
        assert self.n_recv <= NRECV
        return self.n_recv - 1

    def copy(self, src, dst, sent, got, device):
        return pltpu.make_async_remote_copy(
            src_ref=src,
            dst_ref=dst,
            send_sem=self.send.at[sent],
            recv_sem=self.recv.at[got],
            device_id=device,
            device_id_type=MESH,
        )

    def got(self, ref, slot):
        self.copy(ref, ref, 0, slot, self.anyone).wait_recv()

    def sent(self, ref, slot):
        self.copy(ref, ref, slot, 0, self.anyone).wait_send()


def kernel(
    x_hbm, s_hbm, n_hbm,
    xf, xs, pb, px, pr, py, pc, sc, hl, part, rx1, rx2, rz1, rz2, full,
    send_sem, recv_sem, load_sem, panel_sem, out_sem,
):
    layer = lax.axis_index("layer")
    row = lax.axis_index("row")
    col = lax.axis_index("col")
    y, q = lax.div(row, 2), lax.rem(row, 2)
    zh, x = lax.div(col, 4), lax.rem(col, 4)
    owner_core = lax.div(x, 2)
    half = lax.rem(x, 2)

    def m8(value, n):
        return pl.ds(pl.multiple_of(value, 16), n)

    def at_x(d):
        return {"col": zh * 4 + lax.rem(x + d, 4)}

    def at_z(d):
        return {"col": lax.rem(zh + d, 4) * 4 + x}

    def at_y(d):
        return {"row": lax.rem(y + d, 4) * 2 + q}

    partner = {"row": y * 2 + 1 - q}
    sems = Sems(send_sem, recv_sem, partner)
    fetches = q == owner_core
    has_panel = col == 0
    holds = jnp.logical_and(zh == 0, fetches)
    source_0 = jnp.logical_and(has_panel, q == 0)
    source_1 = jnp.logical_and(has_panel, q == 1)
    relay_1 = jnp.logical_and(jnp.logical_and(zh == 0, q == 1), x == 1)
    relay_3 = jnp.logical_and(jnp.logical_and(zh == 0, q == 1), x == 3)

    loads = [
        pltpu.make_async_copy(
            x_hbm.at[pl.ds(i * STEP, STEP), :], xf.at[pl.ds(i * STEP, STEP), :], load_sem.at[i]
        )
        for i in range(ROWS // STEP)
    ]
    panel_loads = [
        pltpu.make_async_copy(
            x_hbm.at[:, pl.ds(pl.multiple_of(layer * (CHUNKS * W) + k * W, W), W)],
            pb.at[k],
            panel_sem.at[k],
        )
        for k in range(CHUNKS)
    ]

    @pl.when(has_panel)
    def _():
        for load in panel_loads:
            load.start()

    for load in loads:
        load.start()

    barrier = pltpu.get_barrier_semaphore()
    greeted = [at_x(1), at_x(3), partner] + [at(d) for at in (at_z, at_y) for d in (1, 2, 3)]
    for device in greeted:
        pl.semaphore_signal(barrier, inc=1, device_id=device, device_id_type=MESH)
    pl.semaphore_wait(barrier, len(greeted))

    def owned(d):
        u = lax.rem(x + d - 2 * q + 4, 4)
        return (2 * lax.rem(lax.div(u + 1, 2), 2) + lax.div(u, 2)) * SLICE

    x_rows = [owned(d) for d in range(4)]

    def z_rows(d):
        return x_rows[0] + lax.rem(zh + d, 4) * SUB

    def reduce_start(buf, r1, rows, size, at, sent, got):
        h = size // 2
        sems.copy(buf.at[m8(rows[2], h)], r1.at[0], sent, got, at(1)).start()
        sems.copy(buf.at[m8(rows[2] + h, h)], r1.at[1], sent, got, at(3)).start()

    def reduce_own(buf, r2, rows, size, at, sent, got):
        h = size // 2
        sems.copy(buf.at[m8(rows[1] + h, h)], r2.at[0, pl.ds(h, h)], sent, got, at(1)).start()
        sems.copy(buf.at[m8(rows[3], h)], r2.at[1, pl.ds(0, h)], sent, got, at(3)).start()

    def reduce_middle(buf, r1, r2, rows, size, at, sent, first, got):
        h = size // 2
        sems.got(r1, first)
        buf[m8(rows[1], h)] += r1[0]
        sems.copy(buf.at[m8(rows[1], h)], r2.at[0, pl.ds(0, h)], sent, got, at(1)).start()
        buf[m8(rows[3] + h, h)] += r1[1]
        sems.copy(buf.at[m8(rows[3] + h, h)], r2.at[1, pl.ds(h, h)], sent, got, at(3)).start()

    def gather_start(buf, rows, size, at, sent, got):
        own = buf.at[m8(rows[0], size)]
        sems.copy(own, own, sent, got, at(1)).start()
        sems.copy(own, own, sent, got, at(3)).start()

    def gather_middle(buf, rows, size, at, sent, first, got):
        h = size // 2
        sems.got(buf.at[pl.ds(0, 2 * size)], first)
        left, right = buf.at[m8(rows[3], h)], buf.at[m8(rows[1] + h, h)]
        sems.copy(left, left, sent, got, at(1)).start()
        sems.copy(right, right, sent, got, at(3)).start()

    def split_rhs(src, k):
        def tile(i, carry):
            rows = pl.ds(pl.multiple_of(i * TILE, TILE), TILE)
            value = src[rows, :]
            hi = value.astype(BF16)
            hl[k, rows, pl.ds(0, W)] = hi
            hl[k, rows, pl.ds(W, W)] = (value - hi.astype(F32)).astype(BF16)
            return carry

        lax.fori_loop(0, DEPTH // TILE, tile, 0)

    def product(buf, k, first_row):
        def tile(i, carry):
            start = first_row + i * TILE
            both = jnp.dot(
                xs[pl.ds(pl.multiple_of(2 * start, 2 * TILE), 2 * TILE), :],
                hl[k],
                preferred_element_type=F32,
            )
            low = both[:TILE, W:] + (both[TILE:, :W] + both[TILE:, W:])
            buf[pl.ds(pl.multiple_of(start, TILE), TILE), :] = both[:TILE, :W] + low
            return carry

        lax.fori_loop(0, SLICE // TILE, tile, 0)

    def minus_panel(buf, k, first_row):
        @pl.when(has_panel)
        def _():
            rows = m8(first_row, SLICE)
            buf[rows, :] -= 3.0 * pb[k, rows, :]

    def split_block(first, last):
        for load in loads[first:last]:
            load.wait()

        def tile(i, carry):
            value = xf[pl.ds(pl.multiple_of(i * 64, 64), 64), :]
            hi = value.astype(BF16)
            to = lax.div(i, TILE // 64) * (2 * TILE) + lax.rem(i, TILE // 64) * 64
            xs[pl.ds(pl.multiple_of(to, 64), 64), :] = hi
            xs[pl.ds(pl.multiple_of(to + TILE, 64), 64), :] = (value - hi.astype(F32)).astype(BF16)
            return carry

        lax.fori_loop(first * STEP // 64, last * STEP // 64, tile, 0)

    def chain(k):
        steps = []
        state = {}

        along_x = [sems.new_recv() for _ in range(4)]
        to_relay = [sems.new_recv() for _ in range(2)]
        scattered = [sems.new_recv() for _ in range(4)][0]
        arrive = sems.new_recv()
        ring = [None] + [sems.new_recv() for _ in range(3)]
        share = sems.new_recv()
        source_sent, relay_sent, scatter_sent, z_sent, ring_sent, share_sent = [
            sems.new_send() for _ in range(6)
        ]

        def piece(ref, i):
            return ref.at[k, pl.ds(i * QUARTER, QUARTER)]

        def from_source(i):
            return sems.copy(piece(pb, 4 + i), piece(px, i), source_sent, along_x[i], at_x(1))

        def from_source_left(i):
            return sems.copy(piece(pb, 4 + i), piece(px, i), source_sent, along_x[i], at_x(3))

        def to_relay_copy(i):
            return sems.copy(piece(pb, i), piece(pr, i % 2), source_sent, to_relay[i % 2], at_x(1 if i < 2 else 3))

        def relay_copy(i):
            return sems.copy(piece(pr, i % 2), piece(px, i), relay_sent, along_x[i], at_x(1 if i < 2 else 3))

        def scatter_copy(i):
            return sems.copy(piece(px, i), py.at[k, y], scatter_sent, scattered + y, {"row": 2 * i + q})

        def z_copy(src, s):
            return sems.copy(src, pc.at[k, mine(0)], z_sent, arrive, {"col": s * 4 + x})

        def panel_send():
            @pl.when(has_panel)
            def _():
                panel_loads[k].wait()

            @pl.when(source_0)
            def _():
                for i in range(4):
                    from_source(i).start()
                px[k] = pb[k, pl.ds(0, DEPTH)]

            @pl.when(source_1)
            def _():
                for i in (0, 2, 1, 3):
                    to_relay_copy(i).start()
                for i in range(4):
                    from_source_left(i).start()

        def panel_scatter():
            @pl.when(relay_1)
            def _():
                for i in (0, 1):
                    to_relay_copy(i).wait_recv()
                    relay_copy(i).start()

            @pl.when(relay_3)
            def _():
                for i in (2, 3):
                    to_relay_copy(i).wait_recv()
                    relay_copy(i).start()

            @pl.when(holds)
            def _():
                for i in range(4):

                    @pl.when(x != 0)
                    def _(i=i):
                        from_source(i).wait_recv()

                    @pl.when(y != i)
                    def _(i=i):
                        scatter_copy(i).start()

                    if k == 0:
                        split_block(2 * i, 2 * i + 2)

        def panel_along_z():
            @pl.when(holds)
            def _():
                for s in (2, 1, 3, 0):

                    @pl.when(y != s)
                    def _(s=s):
                        sems.got(py.at[k, s], scattered + s)
                        if s:
                            z_copy(py.at[k, s], s).start()
                        else:
                            pc[k, mine(0)] = py[k, 0]

                    @pl.when(y == s)
                    def _(s=s):
                        if s:
                            z_copy(piece(px, s), s).start()
                        else:
                            pc[k, mine(0)] = px[k, pl.ds(0, QUARTER)]

        def mine(d):
            return m8(lax.rem(y + 4 - d, 4) * QUARTER, QUARTER)

        def ring_copy(d):
            return sems.copy(pc.at[k, mine(0)], pc.at[k, mine(0)], ring_sent, ring[d], at_y(d))

        def share_copy(d):
            return sems.copy(pc.at[k, mine(d)], pc.at[k, mine(d)], share_sent, share, partner)

        def panel_ring():
            @pl.when(fetches)
            def _():
                @pl.when(zh != 0)
                def _():
                    sems.got(pc.at[k, mine(0)], arrive)

                for d in (1, 3, 2):
                    ring_copy(d).start()
                share_copy(0).start()

        def panel_share():
            @pl.when(fetches)
            def _():
                for d in (1, 3, 2):
                    ring_copy(d).wait_recv()
                    share_copy(d).start()

            @pl.when(jnp.logical_not(fetches))
            def _():
                sems.got(pc.at[k], share)

        def panel_drain():
            @pl.when(source_0)
            def _():
                sems.sent(px.at[k], source_sent)

            @pl.when(source_1)
            def _():
                sems.sent(pb.at[k], source_sent)

            @pl.when(jnp.logical_or(relay_1, relay_3))
            def _():
                sems.sent(pr.at[k], relay_sent)

            @pl.when(holds)
            def _():
                sems.sent(px.at[k, pl.ds(0, 3 * QUARTER)], scatter_sent)
                sems.sent(px.at[k, pl.ds(0, 3 * QUARTER)], z_sent)

            @pl.when(fetches)
            def _():
                sems.sent(pc.at[k, pl.ds(0, 3 * QUARTER)], ring_sent)
                sems.sent(pc.at[k], share_sent)

        def ring_drain(phase):
            x_rows_sent = part.at[phase, k, pl.ds(0, 3 * SLICE)]
            sems.sent(x_rows_sent, x_sent[phase])
            sems.sent(x_rows_sent, gx_sent[phase])
            sems.sent(part.at[phase, k, pl.ds(0, 6 * SUB)], z_ring_sent[phase])

        x_sent = [sems.new_send() for _ in range(2)]
        gx_sent = [sems.new_send() for _ in range(2)]
        z_ring_sent = [sems.new_send() for _ in range(2)]
        slots = {
            (phase, u, name): sems.new_recv()
            for phase in range(2)
            for u in range(UNITS)
            for name in ("x1", "x2", "z1", "z2", "g1", "g2", "g3", "g4")
        }

        def multiply(phase):
            buf = part.at[phase, k]

            def run(first_row):
                product(buf, k, first_row)
                if phase == 1:
                    minus_panel(buf, k, first_row)

            def step():
                split_rhs((pc if phase == 0 else sc).at[k], k)
                run(x_rows[2])
                for u in range(UNITS):
                    reduce_start(
                        buf, rx1.at[phase, k, u], unit_x[u], US, at_x, x_sent[phase], slots[phase, u, "x1"]
                    )
                run(x_rows[1])
                run(x_rows[3])
                for u in range(UNITS):
                    reduce_own(
                        buf, rx2.at[phase, k, u], unit_x[u], US, at_x, x_sent[phase], slots[phase, u, "x2"]
                    )
                run(x_rows[0])

            return step

        unit_x = [[r + u * US for r in x_rows] for u in range(UNITS)]
        unit_z = [
            [unit_x[u][0] + lax.rem(zh + d, 4) * UZ for d in range(4)] for u in range(UNITS)
        ]

        def unit_steps(phase, u):
            buf = part.at[phase, k]
            out = full.at[phase, k]
            xr, zr = unit_x[u], unit_z[u]
            xs_, zs_, gs_ = x_sent[phase], z_ring_sent[phase], gx_sent[phase]
            slot = {name: slots[phase, u, name] for name in ("x1", "x2", "z1", "z2", "g1", "g2", "g3", "g4")}

            def x_middle():
                reduce_middle(
                    buf, rx1.at[phase, k, u], rx2.at[phase, k, u], xr, US, at_x, xs_, slot["x1"], slot["x2"]
                )

            def x_end():
                sems.got(rx2.at[phase, k, u], slot["x2"])
                rows = m8(xr[0], US)
                buf[rows] += rx2[phase, k, u, 0] + rx2[phase, k, u, 1]
                reduce_start(buf, rz1.at[phase, k, u], zr, UZ, at_z, zs_, slot["z1"])
                reduce_own(buf, rz2.at[phase, k, u], zr, UZ, at_z, zs_, slot["z2"])

            def z_middle():
                reduce_middle(
                    buf, rz1.at[phase, k, u], rz2.at[phase, k, u], zr, UZ, at_z, zs_, slot["z1"], slot["z2"]
                )

            def z_end():
                sems.got(rz2.at[phase, k, u], slot["z2"])
                rows = m8(zr[0], UZ)
                total = buf[rows] + (rz2[phase, k, u, 0] + rz2[phase, k, u, 1])
                out[rows] = total if phase == 0 else total * -0.5
                gather_start(out, zr, UZ, at_z, zs_, slot["g1"])

            def gz_middle():
                gather_middle(out, zr, UZ, at_z, zs_, slot["g1"], slot["g2"])

            def gx_start():
                sems.got(out.at[pl.ds(0, UZ)], slot["g2"])
                gather_start(out, xr, US, at_x, gs_, slot["g3"])
                if phase == 0:
                    send_slab(u, 0)

            def gx_middle():
                gather_middle(out, xr, US, at_x, gs_, slot["g3"], slot["g4"])
                if phase == 0:
                    send_slab(u, 1)

            def gx_end():
                sems.got(out.at[pl.ds(0, US)], slot["g4"])
                if u == UNITS - 1:
                    store = pltpu.make_async_copy(
                        out,
                        (s_hbm if phase == 0 else n_hbm).at[:, pl.ds(k * W, W)],
                        out_sem.at[phase, k],
                    )
                    store.start()
                    state[phase, "store"] = store

            return [x_middle, x_end, z_middle, z_end, gz_middle, gx_start, gx_middle, gx_end]

        turn = lax.rem(y - zh + 4, 4)
        root = jnp.logical_and(fetches, turn == 0)
        y1 = jnp.logical_and(fetches, turn == 1)
        y2 = jnp.logical_and(fetches, turn == 2)
        y3 = jnp.logical_and(fetches, turn == 3)
        fwd = {(i, u): sems.new_recv() for i in range(2) for u in range(UNITS)}
        root_sent, onward_sent, across_sent = [sems.new_send() for _ in range(3)]

        def held(i, u):
            return full.at[0, k, m8(half * DEPTH + i * SLICE + u * US, US)]

        def block(i, u):
            return sc.at[k, pl.ds(i * SLICE + u * US, US)]

        def from_root(i, u, d):
            return sems.copy(held(i, u), block(i, u), root_sent, fwd[i, u], at_y(d))

        def onward(i, u):
            return sems.copy(block(i, u), block(i, u), onward_sent, fwd[i, u], at_y(1 + 2 * i))

        def across(i, u):
            return sems.copy(block(i, u), block(i, u), across_sent, fwd[i, u], partner)

        def send_slab(u, i):
            @pl.when(root)
            def _():
                from_root(i, u, 1).start()
                from_root(i, u, 3).start()
                block(i, u)[...] = held(i, u)[...]
                across(i, u).start()

        def pass_slab(u, i):
            def step():
                for d, here in ((1, y1), (3, y3)):

                    @pl.when(here)
                    def _(d=d):
                        from_root(i, u, d).wait_recv()
                        if d == 1 + 2 * i:
                            onward(i, u).start()
                        across(i, u).start()

            return step

        def end_slab(u, i):
            def step():
                @pl.when(y2)
                def _():
                    onward(i, u).wait_recv()
                    across(i, u).start()

                @pl.when(jnp.logical_not(fetches))
                def _():
                    across(i, u).wait_recv()

            return step

        pieces = [(u, i) for u in range(UNITS) for i in range(2)]

        def slab_drain():
            @pl.when(root)
            def _():
                sems.sent(full.at[0, k], root_sent)

            @pl.when(jnp.logical_or(y1, y3))
            def _():
                sems.sent(sc.at[k, pl.ds(0, SLICE)], onward_sent)

            @pl.when(fetches)
            def _():
                sems.sent(sc.at[k], across_sent)

            ring_drain(0)
            ring_drain(1)

        panel = [panel_send, panel_scatter, panel_along_z, panel_ring, panel_share]
        named = {("p", i): f for i, f in enumerate(panel)}
        named["m", 0], named["m", 1] = multiply(0), multiply(1)
        for phase in range(2):
            for u in range(UNITS):
                for i, f in enumerate(unit_steps(phase, u)):
                    named["u", phase, u, i] = f
        for u, i in pieces:
            named["s", u, i] = pass_slab(u, i)
            named["e", u, i] = end_slab(u, i)
        return named, [panel_drain, slab_drain], state

    chains = [chain(k) for k in range(CHUNKS)]
    for step in ORDER:
        if step == "split":

            @pl.when(jnp.logical_not(holds))
            def _():
                split_block(0, ROWS // STEP)
        else:
            chains[step[0]][0][step[1:]]()
    for _, ends, state in chains:
        for end in ends:
            end()
        for phase in range(2):
            state[phase, "store"].wait()


def solution(mesh):
    def body(matrix):
        return pl.pallas_call(
            kernel,
            out_shape=(
                jax.ShapeDtypeStruct((ROWS, CHUNKS * W), F32),
                jax.ShapeDtypeStruct((ROWS, CHUNKS * W), F32),
            ),
            in_specs=[pl.BlockSpec(memory_space=pl.ANY)],
            out_specs=(pl.BlockSpec(memory_space=pl.ANY), pl.BlockSpec(memory_space=pl.ANY)),
            scratch_shapes=[
                pltpu.VMEM((ROWS, DEPTH), F32),
                pltpu.VMEM((2 * ROWS, DEPTH), BF16),
                pltpu.VMEM((CHUNKS, ROWS, W), F32),
                pltpu.VMEM((CHUNKS, DEPTH, W), F32),
                pltpu.VMEM((CHUNKS, 2 * QUARTER, W), F32),
                pltpu.VMEM((CHUNKS, 4, QUARTER, W), F32),
                pltpu.VMEM((CHUNKS, DEPTH, W), F32),
                pltpu.VMEM((CHUNKS, DEPTH, W), F32),
                pltpu.VMEM((CHUNKS, DEPTH, 2 * W), BF16),
                pltpu.VMEM((2, CHUNKS, ROWS, W), F32),
                pltpu.VMEM((2, CHUNKS, UNITS, 2, US // 2, W), F32),
                pltpu.VMEM((2, CHUNKS, UNITS, 2, US, W), F32),
                pltpu.VMEM((2, CHUNKS, UNITS, 2, UZ // 2, W), F32),
                pltpu.VMEM((2, CHUNKS, UNITS, 2, UZ, W), F32),
                pltpu.VMEM((2, CHUNKS, ROWS, W), F32),
                pltpu.SemaphoreType.DMA((NSEND,)),
                pltpu.SemaphoreType.DMA((NRECV,)),
                pltpu.SemaphoreType.DMA((ROWS // STEP,)),
                pltpu.SemaphoreType.DMA((CHUNKS,)),
                pltpu.SemaphoreType.DMA((2, CHUNKS)),
            ],
            compiler_params=pltpu.CompilerParams(
                collective_id=0, has_side_effects=True, vmem_limit_bytes=60 * 1024 * 1024
            ),
        )(matrix)

    return jax.shard_map(
        body,
        mesh=mesh,
        in_specs=(P("row", "col"),),
        out_specs=(P("row", "layer"), P("row", "layer")),
        check_vma=False,
    )
```

```python
import functools

import jax
import jax.numpy as jnp
from jax import lax
from jax.experimental import pallas as pl
from jax.experimental.pallas import tpu as pltpu
from jax.sharding import PartitionSpec as P

MESH = pl.DeviceIdType.MESH
F32 = jnp.float32
BF16 = jnp.bfloat16

CHUNKS = 2
W = 128
ROWS = 2048
DEPTH = 1024
SLICE = 512
SUB = 128
TILE = 512
QUARTER = 256
STEP = 256
NRECV = CHUNKS * (15 + 18 * 4)
NSEND = CHUNKS * 15
UNITS = 4
US = 512 // UNITS
UZ = 128 // UNITS


ORDER = (
    (0, "p", 0), (1, "p", 0), "split", (0, "p", 1), (0, "p", 2), (1, "p", 1), (1, "p", 2), (0, "p", 3), (0, "p", 4),
    (0, "m", 0), (1, "p", 3), (0, "u", 0, 0, 0), (0, "u", 0, 1, 0), (0, "u", 0, 2, 0), (0, "u", 0, 3, 0), (1, "p", 4),
    (0, "u", 0, 0, 1), (0, "u", 0, 1, 1), (1, "m", 0), (0, "u", 0, 2, 1), (0, "u", 0, 3, 1), (0, "u", 0, 0, 2),
    (0, "u", 0, 1, 2), (1, "u", 0, 0, 0), (1, "u", 0, 1, 0), (1, "u", 0, 2, 0), (1, "u", 0, 3, 0), (0, "u", 0, 2, 2),
    (0, "u", 0, 3, 2), (0, "u", 0, 0, 3), (0, "u", 0, 1, 3), (1, "u", 0, 0, 1), (1, "u", 0, 1, 1), (1, "u", 0, 2, 1),
    (0, "u", 0, 2, 3), (1, "u", 0, 3, 1), (0, "u", 0, 3, 3), (0, "u", 0, 0, 4), (0, "u", 0, 1, 4), (1, "u", 0, 0, 2),
    (1, "u", 0, 1, 2), (1, "u", 0, 2, 2), (0, "u", 0, 2, 4), (1, "u", 0, 3, 2), (0, "u", 0, 3, 4), (0, "u", 0, 0, 5),
    (0, "u", 0, 1, 5), (1, "u", 0, 0, 3), (1, "u", 0, 1, 3), (1, "u", 0, 2, 3), (0, "u", 0, 2, 5), (1, "u", 0, 3, 3),
    (0, "s", 0, 0), (0, "u", 0, 3, 5), (0, "s", 1, 0), (0, "u", 0, 0, 6), (0, "s", 2, 0), (1, "u", 0, 0, 4),
    (0, "u", 0, 1, 6), (0, "e", 0, 0), (1, "u", 0, 1, 4), (0, "s", 3, 0), (0, "e", 1, 0), (1, "u", 0, 2, 4),
    (0, "s", 0, 1), (0, "u", 0, 2, 6), (1, "u", 0, 3, 4), (0, "e", 2, 0), (0, "s", 1, 1), (0, "u", 0, 3, 6),
    (1, "u", 0, 0, 5), (0, "e", 3, 0), (0, "u", 0, 0, 7), (1, "u", 0, 1, 5), (0, "e", 0, 1), (0, "s", 2, 1),
    (0, "u", 0, 1, 7), (1, "u", 0, 2, 5), (0, "u", 0, 2, 7), (1, "u", 0, 3, 5), (0, "e", 1, 1), (0, "s", 3, 1),
    (0, "u", 0, 3, 7), (1, "s", 0, 0), (0, "e", 2, 1), (1, "s", 1, 0), (1, "u", 0, 0, 6), (1, "s", 2, 0),
    (0, "e", 3, 1), (1, "s", 3, 0), (1, "u", 0, 1, 6), (1, "e", 0, 0), (0, "m", 1), (1, "e", 1, 0), (1, "s", 0, 1),
    (1, "u", 0, 2, 6), (1, "e", 2, 0), (1, "e", 3, 0), (1, "s", 1, 1), (1, "u", 0, 3, 6), (1, "u", 0, 0, 7),
    (1, "u", 0, 1, 7), (0, "u", 1, 0, 0), (0, "u", 1, 1, 0), (0, "u", 1, 2, 0), (0, "u", 1, 3, 0), (1, "e", 0, 1),
    (1, "s", 2, 1), (1, "e", 1, 1), (1, "s", 3, 1), (1, "e", 2, 1), (1, "u", 0, 2, 7), (1, "e", 3, 1),
    (1, "u", 0, 3, 7), (0, "u", 1, 0, 1), (1, "m", 1), (0, "u", 1, 1, 1), (0, "u", 1, 2, 1), (0, "u", 1, 3, 1),
    (0, "u", 1, 0, 2), (1, "u", 1, 0, 0), (1, "u", 1, 1, 0), (1, "u", 1, 2, 0), (1, "u", 1, 3, 0), (0, "u", 1, 1, 2),
    (0, "u", 1, 2, 2), (0, "u", 1, 3, 2), (1, "u", 1, 0, 1), (0, "u", 1, 0, 3), (1, "u", 1, 1, 1), (1, "u", 1, 2, 1),
    (0, "u", 1, 1, 3), (1, "u", 1, 3, 1), (0, "u", 1, 2, 3), (0, "u", 1, 3, 3), (1, "u", 1, 0, 2), (0, "u", 1, 0, 4),
    (1, "u", 1, 1, 2), (1, "u", 1, 2, 2), (0, "u", 1, 1, 4), (1, "u", 1, 3, 2), (0, "u", 1, 2, 4), (0, "u", 1, 3, 4),
    (1, "u", 1, 0, 3), (0, "u", 1, 0, 5), (1, "u", 1, 1, 3), (1, "u", 1, 2, 3), (0, "u", 1, 1, 5), (1, "u", 1, 3, 3),
    (0, "u", 1, 2, 5), (0, "u", 1, 3, 5), (1, "u", 1, 0, 4), (0, "u", 1, 0, 6), (1, "u", 1, 1, 4), (1, "u", 1, 2, 4),
    (0, "u", 1, 1, 6), (1, "u", 1, 3, 4), (0, "u", 1, 2, 6), (1, "u", 1, 0, 5), (1, "u", 1, 1, 5), (0, "u", 1, 3, 6),
    (1, "u", 1, 2, 5), (0, "u", 1, 0, 7), (1, "u", 1, 3, 5), (0, "u", 1, 1, 7), (0, "u", 1, 2, 7), (1, "u", 1, 0, 6),
    (1, "u", 1, 1, 6), (0, "u", 1, 3, 7), (1, "u", 1, 2, 6), (1, "u", 1, 3, 6), (1, "u", 1, 0, 7), (1, "u", 1, 1, 7),
    (1, "u", 1, 2, 7), (1, "u", 1, 3, 7),
)


class Sems:
    def __init__(self, send, recv, anyone):
        self.send, self.recv, self.anyone, self.n_send, self.n_recv = send, recv, anyone, 0, 0

    def new_send(self):
        self.n_send += 1
        assert self.n_send <= NSEND
        return self.n_send - 1

    def new_recv(self):
        self.n_recv += 1
        assert self.n_recv <= NRECV
        return self.n_recv - 1

    def copy(self, src, dst, sent, got, device):
        return pltpu.make_async_remote_copy(
            src_ref=src,
            dst_ref=dst,
            send_sem=self.send.at[sent],
            recv_sem=self.recv.at[got],
            device_id=device,
            device_id_type=MESH,
        )

    def got(self, ref, slot):
        self.copy(ref, ref, 0, slot, self.anyone).wait_recv()

    def sent(self, ref, slot):
        self.copy(ref, ref, slot, 0, self.anyone).wait_send()


def kernel(
    x_hbm, s_out, n_out,
    xf, xs, pb, px, pr, py, pc, sc, hl, part, rx1, rx2, rz1, rz2,
    send_sem, recv_sem, load_sem, panel_sem,
):
    outs = (s_out, n_out)
    layer = lax.axis_index("layer")
    row = lax.axis_index("row")
    col = lax.axis_index("col")
    y, q = lax.div(row, 2), lax.rem(row, 2)
    zh, x = lax.div(col, 4), lax.rem(col, 4)
    owner_core = lax.div(x, 2)
    half = lax.rem(x, 2)

    def m8(value, n):
        return pl.ds(pl.multiple_of(value, 16), n)

    def at_x(d):
        return {"col": zh * 4 + lax.rem(x + d, 4)}

    def at_z(d):
        return {"col": lax.rem(zh + d, 4) * 4 + x}

    def at_y(d):
        return {"row": lax.rem(y + d, 4) * 2 + q}

    partner = {"row": y * 2 + 1 - q}
    sems = Sems(send_sem, recv_sem, partner)
    fetches = q == owner_core
    has_panel = col == 0
    holds = jnp.logical_and(zh == 0, fetches)
    source_0 = jnp.logical_and(has_panel, q == 0)
    source_1 = jnp.logical_and(has_panel, q == 1)
    relay_1 = jnp.logical_and(jnp.logical_and(zh == 0, q == 1), x == 1)
    relay_3 = jnp.logical_and(jnp.logical_and(zh == 0, q == 1), x == 3)

    loads = [
        pltpu.make_async_copy(
            x_hbm.at[pl.ds(i * STEP, STEP), :], xf.at[pl.ds(i * STEP, STEP), :], load_sem.at[i]
        )
        for i in range(ROWS // STEP)
    ]
    panel_loads = [
        pltpu.make_async_copy(
            x_hbm.at[:, pl.ds(pl.multiple_of(layer * (CHUNKS * W) + k * W, W), W)],
            pb.at[k],
            panel_sem.at[k],
        )
        for k in range(CHUNKS)
    ]

    @pl.when(has_panel)
    def _():
        for load in panel_loads:
            load.start()

    for load in loads:
        load.start()

    barrier = pltpu.get_barrier_semaphore()
    greeted = [at_x(1), at_x(3), partner] + [at(d) for at in (at_z, at_y) for d in (1, 2, 3)]
    for device in greeted:
        pl.semaphore_signal(barrier, inc=1, device_id=device, device_id_type=MESH)
    pl.semaphore_wait(barrier, len(greeted))

    def owned(d):
        u = lax.rem(x + d - 2 * q + 4, 4)
        return (2 * lax.rem(lax.div(u + 1, 2), 2) + lax.div(u, 2)) * SLICE

    x_rows = [owned(d) for d in range(4)]

    def z_rows(d):
        return x_rows[0] + lax.rem(zh + d, 4) * SUB

    def reduce_start(buf, r1, rows, size, at, sent, got):
        h = size // 2
        sems.copy(buf.at[m8(rows[2], h)], r1.at[0], sent, got, at(1)).start()
        sems.copy(buf.at[m8(rows[2] + h, h)], r1.at[1], sent, got, at(3)).start()

    def reduce_own(buf, r2, rows, size, at, sent, got):
        h = size // 2
        sems.copy(buf.at[m8(rows[1] + h, h)], r2.at[0, pl.ds(h, h)], sent, got, at(1)).start()
        sems.copy(buf.at[m8(rows[3], h)], r2.at[1, pl.ds(0, h)], sent, got, at(3)).start()

    def reduce_middle(buf, r1, r2, rows, size, at, sent, first, got):
        h = size // 2
        sems.got(r1, first)
        buf[m8(rows[1], h)] += r1[0]
        sems.copy(buf.at[m8(rows[1], h)], r2.at[0, pl.ds(0, h)], sent, got, at(1)).start()
        buf[m8(rows[3] + h, h)] += r1[1]
        sems.copy(buf.at[m8(rows[3] + h, h)], r2.at[1, pl.ds(h, h)], sent, got, at(3)).start()

    def gather_start(buf, rows, size, at, sent, got):
        own = buf.at[m8(rows[0], size)]
        sems.copy(own, own, sent, got, at(1)).start()
        sems.copy(own, own, sent, got, at(3)).start()

    def gather_middle(buf, rows, size, at, sent, first, got):
        h = size // 2
        sems.got(buf.at[pl.ds(0, 2 * size)], first)
        left, right = buf.at[m8(rows[3], h)], buf.at[m8(rows[1] + h, h)]
        sems.copy(left, left, sent, got, at(1)).start()
        sems.copy(right, right, sent, got, at(3)).start()

    def split_rhs(src, k):
        def tile(i, carry):
            rows = pl.ds(pl.multiple_of(i * TILE, TILE), TILE)
            value = src[rows, :]
            hi = value.astype(BF16)
            hl[k, rows, pl.ds(0, W)] = hi
            hl[k, rows, pl.ds(W, W)] = (value - hi.astype(F32)).astype(BF16)
            return carry

        lax.fori_loop(0, DEPTH // TILE, tile, 0)

    def product(buf, k, first_row):
        def tile(i, carry):
            start = first_row + i * TILE
            both = jnp.dot(
                xs[pl.ds(pl.multiple_of(2 * start, 2 * TILE), 2 * TILE), :],
                hl[k],
                preferred_element_type=F32,
            )
            low = both[:TILE, W:] + (both[TILE:, :W] + both[TILE:, W:])
            buf[pl.ds(pl.multiple_of(start, TILE), TILE), :] = both[:TILE, :W] + low
            return carry

        lax.fori_loop(0, SLICE // TILE, tile, 0)

    def minus_panel(buf, k, first_row):
        @pl.when(has_panel)
        def _():
            rows = m8(first_row, SLICE)
            buf[rows, :] -= 3.0 * pb[k, rows, :]

    def split_block(first, last):
        for load in loads[first:last]:
            load.wait()

        def tile(i, carry):
            value = xf[pl.ds(pl.multiple_of(i * 64, 64), 64), :]
            hi = value.astype(BF16)
            to = lax.div(i, TILE // 64) * (2 * TILE) + lax.rem(i, TILE // 64) * 64
            xs[pl.ds(pl.multiple_of(to, 64), 64), :] = hi
            xs[pl.ds(pl.multiple_of(to + TILE, 64), 64), :] = (value - hi.astype(F32)).astype(BF16)
            return carry

        lax.fori_loop(first * STEP // 64, last * STEP // 64, tile, 0)

    def chain(k):
        steps = []
        state = {}

        along_x = [sems.new_recv() for _ in range(4)]
        to_relay = [sems.new_recv() for _ in range(2)]
        scattered = [sems.new_recv() for _ in range(4)][0]
        arrive = sems.new_recv()
        ring = [None] + [sems.new_recv() for _ in range(3)]
        share = sems.new_recv()
        source_sent, relay_sent, scatter_sent, z_sent, ring_sent, share_sent = [
            sems.new_send() for _ in range(6)
        ]

        def piece(ref, i):
            return ref.at[k, pl.ds(i * QUARTER, QUARTER)]

        def from_source(i):
            return sems.copy(piece(pb, 4 + i), piece(px, i), source_sent, along_x[i], at_x(1))

        def from_source_left(i):
            return sems.copy(piece(pb, 4 + i), piece(px, i), source_sent, along_x[i], at_x(3))

        def to_relay_copy(i):
            return sems.copy(piece(pb, i), piece(pr, i % 2), source_sent, to_relay[i % 2], at_x(1 if i < 2 else 3))

        def relay_copy(i):
            return sems.copy(piece(pr, i % 2), piece(px, i), relay_sent, along_x[i], at_x(1 if i < 2 else 3))

        def scatter_copy(i):
            return sems.copy(piece(px, i), py.at[k, y], scatter_sent, scattered + y, {"row": 2 * i + q})

        def z_copy(src, s):
            return sems.copy(src, pc.at[k, mine(0)], z_sent, arrive, {"col": s * 4 + x})

        def panel_send():
            @pl.when(has_panel)
            def _():
                panel_loads[k].wait()

            @pl.when(source_0)
            def _():
                for i in range(4):
                    from_source(i).start()
                px[k] = pb[k, pl.ds(0, DEPTH)]

            @pl.when(source_1)
            def _():
                for i in (0, 2, 1, 3):
                    to_relay_copy(i).start()
                for i in range(4):
                    from_source_left(i).start()

        def panel_scatter():
            @pl.when(relay_1)
            def _():
                for i in (0, 1):
                    to_relay_copy(i).wait_recv()
                    relay_copy(i).start()

            @pl.when(relay_3)
            def _():
                for i in (2, 3):
                    to_relay_copy(i).wait_recv()
                    relay_copy(i).start()

            @pl.when(holds)
            def _():
                for i in range(4):

                    @pl.when(x != 0)
                    def _(i=i):
                        from_source(i).wait_recv()

                    @pl.when(y != i)
                    def _(i=i):
                        scatter_copy(i).start()

                    if k == 0:
                        split_block(2 * i, 2 * i + 2)

        def panel_along_z():
            @pl.when(holds)
            def _():
                for s in (2, 1, 3, 0):

                    @pl.when(y != s)
                    def _(s=s):
                        sems.got(py.at[k, s], scattered + s)
                        if s:
                            z_copy(py.at[k, s], s).start()
                        else:
                            pc[k, mine(0)] = py[k, 0]

                    @pl.when(y == s)
                    def _(s=s):
                        if s:
                            z_copy(piece(px, s), s).start()
                        else:
                            pc[k, mine(0)] = px[k, pl.ds(0, QUARTER)]

        def mine(d):
            return m8(lax.rem(y + 4 - d, 4) * QUARTER, QUARTER)

        def ring_copy(d):
            return sems.copy(pc.at[k, mine(0)], pc.at[k, mine(0)], ring_sent, ring[d], at_y(d))

        def share_copy(d):
            return sems.copy(pc.at[k, mine(d)], pc.at[k, mine(d)], share_sent, share, partner)

        def panel_ring():
            @pl.when(fetches)
            def _():
                @pl.when(zh != 0)
                def _():
                    sems.got(pc.at[k, mine(0)], arrive)

                for d in (2, 1, 3):
                    ring_copy(d).start()
                share_copy(0).start()

        def panel_share():
            @pl.when(fetches)
            def _():
                for d in (1, 3, 2):
                    ring_copy(d).wait_recv()
                    share_copy(d).start()

            @pl.when(jnp.logical_not(fetches))
            def _():
                sems.got(pc.at[k], share)

        def panel_drain():
            @pl.when(source_0)
            def _():
                sems.sent(px.at[k], source_sent)

            @pl.when(source_1)
            def _():
                sems.sent(pb.at[k], source_sent)

            @pl.when(jnp.logical_or(relay_1, relay_3))
            def _():
                sems.sent(pr.at[k], relay_sent)

            @pl.when(holds)
            def _():
                sems.sent(px.at[k, pl.ds(0, 3 * QUARTER)], scatter_sent)
                sems.sent(px.at[k, pl.ds(0, 3 * QUARTER)], z_sent)

            @pl.when(fetches)
            def _():
                sems.sent(pc.at[k, pl.ds(0, 3 * QUARTER)], ring_sent)
                sems.sent(pc.at[k], share_sent)

        def ring_drain(phase):
            x_rows_sent = part.at[phase, k, pl.ds(0, 3 * SLICE)]
            sems.sent(x_rows_sent, x_sent[phase])
            sems.sent(x_rows_sent, gx_sent[phase])
            sems.sent(part.at[phase, k, pl.ds(0, 6 * SUB)], z_ring_sent[phase])

        x_sent = [sems.new_send() for _ in range(2)]
        gx_sent = [sems.new_send() for _ in range(2)]
        z_ring_sent = [sems.new_send() for _ in range(2)]
        slots = {
            (phase, u, name): sems.new_recv()
            for phase in range(2)
            for u in range(UNITS)
            for name in ("x1", "x2", "z1", "z2", "g1", "g2", "g3", "g4")
        }

        def multiply(phase):
            buf = part.at[phase, k]

            def run(first_row):
                product(buf, k, first_row)
                if phase == 1:
                    minus_panel(buf, k, first_row)

            def step():
                split_rhs((pc if phase == 0 else sc).at[k], k)
                run(x_rows[2])
                for u in range(UNITS):
                    reduce_start(
                        buf, rx1.at[phase, k, u], unit_x[u], US, at_x, x_sent[phase], slots[phase, u, "x1"]
                    )
                run(x_rows[1])
                run(x_rows[3])
                for u in range(UNITS):
                    reduce_own(
                        buf, rx2.at[phase, k, u], unit_x[u], US, at_x, x_sent[phase], slots[phase, u, "x2"]
                    )
                run(x_rows[0])

            return step

        unit_x = [[r + u * US for r in x_rows] for u in range(UNITS)]
        unit_z = [
            [unit_x[u][0] + lax.rem(zh + d, 4) * UZ for d in range(4)] for u in range(UNITS)
        ]

        def unit_steps(phase, u):
            buf = part.at[phase, k]
            out = outs[phase].at[k]
            xr, zr = unit_x[u], unit_z[u]
            xs_, zs_, gs_ = x_sent[phase], z_ring_sent[phase], gx_sent[phase]
            slot = {name: slots[phase, u, name] for name in ("x1", "x2", "z1", "z2", "g1", "g2", "g3", "g4")}

            def x_middle():
                reduce_middle(
                    buf, rx1.at[phase, k, u], rx2.at[phase, k, u], xr, US, at_x, xs_, slot["x1"], slot["x2"]
                )

            def x_end():
                sems.got(rx2.at[phase, k, u], slot["x2"])
                rows = m8(xr[0], US)
                buf[rows] += rx2[phase, k, u, 0] + rx2[phase, k, u, 1]
                reduce_start(buf, rz1.at[phase, k, u], zr, UZ, at_z, zs_, slot["z1"])
                reduce_own(buf, rz2.at[phase, k, u], zr, UZ, at_z, zs_, slot["z2"])

            def z_middle():
                reduce_middle(
                    buf, rz1.at[phase, k, u], rz2.at[phase, k, u], zr, UZ, at_z, zs_, slot["z1"], slot["z2"]
                )

            def z_end():
                sems.got(rz2.at[phase, k, u], slot["z2"])
                rows = m8(zr[0], UZ)
                total = buf[rows] + (rz2[phase, k, u, 0] + rz2[phase, k, u, 1])
                out[rows] = total if phase == 0 else total * -0.5
                gather_start(out, zr, UZ, at_z, zs_, slot["g1"])

            def gz_middle():
                gather_middle(out, zr, UZ, at_z, zs_, slot["g1"], slot["g2"])

            def gx_start():
                sems.got(out.at[pl.ds(0, UZ)], slot["g2"])
                gather_start(out, xr, US, at_x, gs_, slot["g3"])
                if phase == 0:
                    send_slab(u, 0)

            def gx_middle():
                gather_middle(out, xr, US, at_x, gs_, slot["g3"], slot["g4"])
                if phase == 0:
                    send_slab(u, 1)

            def gx_end():
                sems.got(out.at[pl.ds(0, US)], slot["g4"])

            return [x_middle, x_end, z_middle, z_end, gz_middle, gx_start, gx_middle, gx_end]

        turn = lax.rem(y - zh + 4, 4)
        root = jnp.logical_and(fetches, turn == 0)
        y1 = jnp.logical_and(fetches, turn == 1)
        y2 = jnp.logical_and(fetches, turn == 2)
        y3 = jnp.logical_and(fetches, turn == 3)
        fwd = {(i, u): sems.new_recv() for i in range(2) for u in range(UNITS)}
        root_sent, onward_sent, across_sent = [sems.new_send() for _ in range(3)]

        def held(i, u):
            return outs[0].at[k, m8(half * DEPTH + i * SLICE + u * US, US)]

        def block(i, u):
            return sc.at[k, pl.ds(i * SLICE + u * US, US)]

        def from_root(i, u, d):
            return sems.copy(held(i, u), block(i, u), root_sent, fwd[i, u], at_y(d))

        def onward(i, u):
            return sems.copy(block(i, u), block(i, u), onward_sent, fwd[i, u], at_y(1 + 2 * i))

        def across(i, u):
            return sems.copy(block(i, u), block(i, u), across_sent, fwd[i, u], partner)

        def send_slab(u, i):
            @pl.when(root)
            def _():
                from_root(i, u, 1).start()
                from_root(i, u, 3).start()
                block(i, u)[...] = held(i, u)[...]
                across(i, u).start()

        def pass_slab(u, i):
            def step():
                for d, here in ((1, y1), (3, y3)):

                    @pl.when(here)
                    def _(d=d):
                        from_root(i, u, d).wait_recv()
                        if d == 1 + 2 * i:
                            onward(i, u).start()
                        across(i, u).start()

            return step

        def end_slab(u, i):
            def step():
                @pl.when(y2)
                def _():
                    onward(i, u).wait_recv()
                    across(i, u).start()

                @pl.when(jnp.logical_not(fetches))
                def _():
                    across(i, u).wait_recv()

            return step

        pieces = [(u, i) for u in range(UNITS) for i in range(2)]

        def slab_drain():
            @pl.when(root)
            def _():
                sems.sent(outs[0].at[k], root_sent)

            @pl.when(jnp.logical_or(y1, y3))
            def _():
                sems.sent(sc.at[k, pl.ds(0, SLICE)], onward_sent)

            @pl.when(fetches)
            def _():
                sems.sent(sc.at[k], across_sent)

            ring_drain(0)
            ring_drain(1)

        panel = [panel_send, panel_scatter, panel_along_z, panel_ring, panel_share]
        named = {("p", i): f for i, f in enumerate(panel)}
        named["m", 0], named["m", 1] = multiply(0), multiply(1)
        for phase in range(2):
            for u in range(UNITS):
                for i, f in enumerate(unit_steps(phase, u)):
                    named["u", phase, u, i] = f
        for u, i in pieces:
            named["s", u, i] = pass_slab(u, i)
            named["e", u, i] = end_slab(u, i)
        return named, [panel_drain, slab_drain], state

    chains = [chain(k) for k in range(CHUNKS)]
    for step in ORDER:
        if step == "split":

            @pl.when(jnp.logical_not(holds))
            def _():
                split_block(0, ROWS // STEP)
        else:
            chains[step[0]][0][step[1:]]()
    for _, ends, state in chains:
        for end in ends:
            end()


def lay_out(square, new, square_out, new_out, sem):
    copies = [
        pltpu.make_async_copy(src.at[k], dst.at[:, pl.ds(k * W, W)], sem.at[i, k])
        for i, (src, dst) in enumerate(((square, square_out), (new, new_out)))
        for k in range(CHUNKS)
    ]
    for copy in copies:
        copy.start()
    for copy in copies:
        copy.wait()


def solution(mesh):
    def body(matrix):
        square, new = pl.pallas_call(
            kernel,
            out_shape=(
                pltpu.VMEM((CHUNKS, ROWS, W), F32),
                pltpu.VMEM((CHUNKS, ROWS, W), F32),
            ),
            in_specs=[pl.BlockSpec(memory_space=pl.ANY)],
            out_specs=(pl.BlockSpec(memory_space=pltpu.VMEM), pl.BlockSpec(memory_space=pltpu.VMEM)),
            scratch_shapes=[
                pltpu.VMEM((ROWS, DEPTH), F32),
                pltpu.VMEM((2 * ROWS, DEPTH), BF16),
                pltpu.VMEM((CHUNKS, ROWS, W), F32),
                pltpu.VMEM((CHUNKS, DEPTH, W), F32),
                pltpu.VMEM((CHUNKS, 2 * QUARTER, W), F32),
                pltpu.VMEM((CHUNKS, 4, QUARTER, W), F32),
                pltpu.VMEM((CHUNKS, DEPTH, W), F32),
                pltpu.VMEM((CHUNKS, DEPTH, W), F32),
                pltpu.VMEM((CHUNKS, DEPTH, 2 * W), BF16),
                pltpu.VMEM((2, CHUNKS, ROWS, W), F32),
                pltpu.VMEM((2, CHUNKS, UNITS, 2, US // 2, W), F32),
                pltpu.VMEM((2, CHUNKS, UNITS, 2, US, W), F32),
                pltpu.VMEM((2, CHUNKS, UNITS, 2, UZ // 2, W), F32),
                pltpu.VMEM((2, CHUNKS, UNITS, 2, UZ, W), F32),
                pltpu.SemaphoreType.DMA((NSEND,)),
                pltpu.SemaphoreType.DMA((NRECV,)),
                pltpu.SemaphoreType.DMA((ROWS // STEP,)),
                pltpu.SemaphoreType.DMA((CHUNKS,)),
            ],
            compiler_params=pltpu.CompilerParams(
                collective_id=0, has_side_effects=True, vmem_limit_bytes=52 * 1024 * 1024
            ),
        )(matrix)
        whole = jax.ShapeDtypeStruct((ROWS, CHUNKS * W), F32)
        anywhere = pl.BlockSpec(memory_space=pl.ANY)
        return pl.pallas_call(
            lay_out,
            out_shape=(whole, whole),
            in_specs=[anywhere, anywhere],
            out_specs=(anywhere, anywhere),
            scratch_shapes=[pltpu.SemaphoreType.DMA((2, CHUNKS))],
            compiler_params=pltpu.CompilerParams(vmem_limit_bytes=1024 * 1024),
        )(square, new)

    return jax.shard_map(
        body,
        mesh=mesh,
        in_specs=(P("row", "col"),),
        out_specs=(P("row", "layer"), P("row", "layer")),
        check_vma=False,
    )
```

```python
import functools

import jax
import jax.numpy as jnp
from jax import lax
from jax.experimental import pallas as pl
from jax.experimental.pallas import tpu as pltpu
from jax.sharding import PartitionSpec as P

MESH = pl.DeviceIdType.MESH
F32 = jnp.float32
BF16 = jnp.bfloat16

CHUNKS = 2
W = 128
ROWS = 2048
DEPTH = 1024
SLICE = 512
SUB = 128
TILE = 512
QUARTER = 256
STEP = 256
NRECV = CHUNKS * (15 + 18 * 4)
NSEND = CHUNKS * 15
UNITS = 4
US = 512 // UNITS
UZ = 128 // UNITS


ORDER = (
    (0, "p", 0), (1, "p", 0), "split", (0, "p", 1), (0, "p", 2), (1, "p", 1), (1, "p", 2), (0, "p", 3), (0, "p", 4),
    (0, "m", 0), (1, "p", 3), (0, "u", 0, 0, 0), (0, "u", 0, 1, 0), (0, "u", 0, 2, 0), (0, "u", 0, 3, 0), (1, "p", 4),
    (0, "u", 0, 0, 1), (0, "u", 0, 1, 1), (1, "m", 0), (0, "u", 0, 2, 1), (0, "u", 0, 3, 1), (0, "u", 0, 0, 2),
    (0, "u", 0, 1, 2), (1, "u", 0, 0, 0), (1, "u", 0, 1, 0), (1, "u", 0, 2, 0), (1, "u", 0, 3, 0), (0, "u", 0, 2, 2),
    (0, "u", 0, 3, 2), (0, "u", 0, 0, 3), (0, "u", 0, 1, 3), (1, "u", 0, 0, 1), (1, "u", 0, 1, 1), (1, "u", 0, 2, 1),
    (0, "u", 0, 2, 3), (1, "u", 0, 3, 1), (0, "u", 0, 3, 3), (0, "u", 0, 0, 4), (0, "u", 0, 1, 4), (1, "u", 0, 0, 2),
    (1, "u", 0, 1, 2), (1, "u", 0, 2, 2), (0, "u", 0, 2, 4), (1, "u", 0, 3, 2), (0, "u", 0, 3, 4), (0, "u", 0, 0, 5),
    (0, "u", 0, 1, 5), (1, "u", 0, 0, 3), (1, "u", 0, 1, 3), (1, "u", 0, 2, 3), (0, "u", 0, 2, 5), (1, "u", 0, 3, 3),
    (0, "s", 0, 0), (0, "u", 0, 3, 5), (0, "s", 1, 0), (0, "u", 0, 0, 6), (0, "s", 2, 0), (1, "u", 0, 0, 4),
    (0, "u", 0, 1, 6), (0, "e", 0, 0), (1, "u", 0, 1, 4), (0, "s", 3, 0), (0, "e", 1, 0), (1, "u", 0, 2, 4),
    (0, "s", 0, 1), (0, "u", 0, 2, 6), (1, "u", 0, 3, 4), (0, "e", 2, 0), (0, "s", 1, 1), (0, "u", 0, 3, 6),
    (1, "u", 0, 0, 5), (0, "e", 3, 0), (1, "u", 0, 1, 5), (0, "e", 0, 1), (0, "s", 2, 1), (1, "u", 0, 2, 5),
    (1, "u", 0, 3, 5), (0, "e", 1, 1), (0, "s", 3, 1), (1, "s", 0, 0), (0, "e", 2, 1), (1, "s", 1, 0),
    (1, "u", 0, 0, 6), (1, "s", 2, 0), (0, "e", 3, 1), (1, "s", 3, 0), (1, "u", 0, 1, 6), (1, "e", 0, 0), (0, "m", 1),
    (1, "e", 1, 0), (1, "s", 0, 1), (1, "u", 0, 2, 6), (1, "e", 2, 0), (1, "e", 3, 0), (1, "s", 1, 1),
    (1, "u", 0, 3, 6), (0, "u", 1, 0, 0), (0, "u", 1, 1, 0), (0, "u", 1, 2, 0), (0, "u", 1, 3, 0), (1, "e", 0, 1),
    (1, "s", 2, 1), (1, "e", 1, 1), (1, "s", 3, 1), (1, "e", 2, 1), (1, "e", 3, 1), (0, "u", 1, 0, 1), (1, "m", 1),
    (0, "u", 1, 1, 1), (0, "u", 1, 2, 1), (0, "u", 1, 3, 1), (0, "u", 0, 0, 8), (0, "u", 0, 1, 8), (0, "u", 0, 2, 8),
    (0, "u", 0, 3, 8), (0, "u", 1, 0, 2), (1, "u", 1, 0, 0), (1, "u", 1, 1, 0), (1, "u", 1, 2, 0), (1, "u", 1, 3, 0),
    (0, "u", 1, 1, 2), (0, "u", 1, 2, 2), (0, "u", 1, 3, 2), (1, "u", 1, 0, 1), (0, "u", 1, 0, 3), (1, "u", 1, 1, 1),
    (1, "u", 1, 2, 1), (0, "u", 1, 1, 3), (1, "u", 1, 3, 1), (1, "u", 0, 0, 8), (1, "u", 0, 1, 8), (1, "u", 0, 2, 8),
    (1, "u", 0, 3, 8), (0, "u", 1, 2, 3), (0, "u", 1, 3, 3), (1, "u", 1, 0, 2), (0, "u", 1, 0, 4), (1, "u", 1, 1, 2),
    (1, "u", 1, 2, 2), (0, "u", 1, 1, 4), (1, "u", 1, 3, 2), (0, "u", 1, 2, 4), (0, "u", 1, 3, 4), (1, "u", 1, 0, 3),
    (0, "u", 1, 0, 5), (1, "u", 1, 1, 3), (1, "u", 1, 2, 3), (0, "u", 1, 1, 5), (1, "u", 1, 3, 3), (0, "u", 1, 2, 5),
    (0, "u", 1, 3, 5), (1, "u", 1, 0, 4), (0, "u", 1, 0, 6), (1, "u", 1, 1, 4), (1, "u", 1, 2, 4), (0, "u", 1, 1, 6),
    (1, "u", 1, 3, 4), (0, "u", 1, 2, 6), (1, "u", 1, 0, 5), (1, "u", 1, 1, 5), (0, "u", 1, 3, 6), (1, "u", 1, 2, 5),
    (0, "u", 1, 0, 7), (1, "u", 1, 3, 5), (0, "u", 1, 1, 7), (0, "u", 1, 2, 7), (1, "u", 1, 0, 6), (1, "u", 1, 1, 6),
    (0, "u", 1, 3, 7), (1, "u", 1, 2, 6), (1, "u", 1, 3, 6), (1, "u", 1, 0, 7), (1, "u", 1, 1, 7), (1, "u", 1, 2, 7),
    (1, "u", 1, 3, 7), (0, "u", 0, 0, 7), (0, "u", 0, 1, 7), (0, "u", 0, 2, 7), (0, "u", 0, 3, 7), (1, "u", 0, 0, 7),
    (1, "u", 0, 1, 7), (1, "u", 0, 2, 7), (1, "u", 0, 3, 7),
)


class Sems:
    def __init__(self, send, recv, anyone):
        self.send, self.recv, self.anyone, self.n_send, self.n_recv = send, recv, anyone, 0, 0

    def new_send(self):
        self.n_send += 1
        assert self.n_send <= NSEND
        return self.n_send - 1

    def new_recv(self):
        self.n_recv += 1
        assert self.n_recv <= NRECV
        return self.n_recv - 1

    def copy(self, src, dst, sent, got, device):
        return pltpu.make_async_remote_copy(
            src_ref=src,
            dst_ref=dst,
            send_sem=self.send.at[sent],
            recv_sem=self.recv.at[got],
            device_id=device,
            device_id_type=MESH,
        )

    def got(self, ref, slot):
        self.copy(ref, ref, 0, slot, self.anyone).wait_recv()

    def sent(self, ref, slot):
        self.copy(ref, ref, slot, 0, self.anyone).wait_send()


def kernel(
    x_hbm, s_out, n_out,
    xf, xs, pb, px, pr, py, pc, sc, hl, part, rx1, rx2, rz1, rz2,
    send_sem, recv_sem, load_sem, panel_sem,
):
    outs = (s_out, n_out)
    layer = lax.axis_index("layer")
    row = lax.axis_index("row")
    col = lax.axis_index("col")
    y, q = lax.div(row, 2), lax.rem(row, 2)
    zh, x = lax.div(col, 4), lax.rem(col, 4)
    owner_core = lax.div(x, 2)
    half = lax.rem(x, 2)

    def m8(value, n):
        return pl.ds(pl.multiple_of(value, 16), n)

    def at_x(d):
        return {"col": zh * 4 + lax.rem(x + d, 4)}

    def at_z(d):
        return {"col": lax.rem(zh + d, 4) * 4 + x}

    def at_y(d):
        return {"row": lax.rem(y + d, 4) * 2 + q}

    partner = {"row": y * 2 + 1 - q}
    sems = Sems(send_sem, recv_sem, partner)
    fetches = q == owner_core
    has_panel = col == 0
    holds = jnp.logical_and(zh == 0, fetches)
    source_0 = jnp.logical_and(has_panel, q == 0)
    source_1 = jnp.logical_and(has_panel, q == 1)
    relay_1 = jnp.logical_and(jnp.logical_and(zh == 0, q == 1), x == 1)
    relay_3 = jnp.logical_and(jnp.logical_and(zh == 0, q == 1), x == 3)

    loads = [
        pltpu.make_async_copy(
            x_hbm.at[pl.ds(i * STEP, STEP), :], xf.at[pl.ds(i * STEP, STEP), :], load_sem.at[i]
        )
        for i in range(ROWS // STEP)
    ]
    panel_loads = [
        pltpu.make_async_copy(
            x_hbm.at[:, pl.ds(pl.multiple_of(layer * (CHUNKS * W) + k * W, W), W)],
            pb.at[k],
            panel_sem.at[k],
        )
        for k in range(CHUNKS)
    ]

    @pl.when(has_panel)
    def _():
        for load in panel_loads:
            load.start()

    for load in loads:
        load.start()

    barrier = pltpu.get_barrier_semaphore()
    greeted = [at_x(1), at_x(3), partner] + [at(d) for at in (at_z, at_y) for d in (1, 2, 3)]
    for device in greeted:
        pl.semaphore_signal(barrier, inc=1, device_id=device, device_id_type=MESH)
    pl.semaphore_wait(barrier, len(greeted))

    def owned(d):
        u = lax.rem(x + d - 2 * q + 4, 4)
        return (2 * lax.rem(lax.div(u + 1, 2), 2) + lax.div(u, 2)) * SLICE

    x_rows = [owned(d) for d in range(4)]

    def z_rows(d):
        return x_rows[0] + lax.rem(zh + d, 4) * SUB

    def reduce_start(buf, r1, rows, size, at, sent, got):
        h = size // 2
        sems.copy(buf.at[m8(rows[2], h)], r1.at[0], sent, got, at(1)).start()
        sems.copy(buf.at[m8(rows[2] + h, h)], r1.at[1], sent, got, at(3)).start()

    def reduce_own(buf, r2, rows, size, at, sent, got):
        h = size // 2
        sems.copy(buf.at[m8(rows[1] + h, h)], r2.at[0, pl.ds(h, h)], sent, got, at(1)).start()
        sems.copy(buf.at[m8(rows[3], h)], r2.at[1, pl.ds(0, h)], sent, got, at(3)).start()

    def reduce_middle(buf, r1, r2, rows, size, at, sent, first, got):
        h = size // 2
        sems.got(r1, first)
        buf[m8(rows[1], h)] += r1[0]
        sems.copy(buf.at[m8(rows[1], h)], r2.at[0, pl.ds(0, h)], sent, got, at(1)).start()
        buf[m8(rows[3] + h, h)] += r1[1]
        sems.copy(buf.at[m8(rows[3] + h, h)], r2.at[1, pl.ds(h, h)], sent, got, at(3)).start()

    def gather_start(buf, rows, size, at, sent, got):
        own = buf.at[m8(rows[0], size)]
        sems.copy(own, own, sent, got, at(1)).start()
        sems.copy(own, own, sent, got, at(3)).start()

    def gather_arrived(buf, size, first):
        sems.got(buf.at[pl.ds(0, 2 * size)], first)

    def gather_onward(buf, rows, size, at, sent, got):
        h = size // 2
        left, right = buf.at[m8(rows[3], h)], buf.at[m8(rows[1] + h, h)]
        sems.copy(left, left, sent, got, at(1)).start()
        sems.copy(right, right, sent, got, at(3)).start()

    def split_rhs(src, k):
        def tile(i, carry):
            rows = pl.ds(pl.multiple_of(i * TILE, TILE), TILE)
            value = src[rows, :]
            hi = value.astype(BF16)
            hl[k, rows, pl.ds(0, W)] = hi
            hl[k, rows, pl.ds(W, W)] = (value - hi.astype(F32)).astype(BF16)
            return carry

        lax.fori_loop(0, DEPTH // TILE, tile, 0)

    def product(buf, k, first_row):
        def tile(i, carry):
            start = first_row + i * TILE
            both = jnp.dot(
                xs[pl.ds(pl.multiple_of(2 * start, 2 * TILE), 2 * TILE), :],
                hl[k],
                preferred_element_type=F32,
            )
            low = both[:TILE, W:] + (both[TILE:, :W] + both[TILE:, W:])
            buf[pl.ds(pl.multiple_of(start, TILE), TILE), :] = both[:TILE, :W] + low
            return carry

        lax.fori_loop(0, SLICE // TILE, tile, 0)

    def minus_panel(buf, k, first_row):
        @pl.when(has_panel)
        def _():
            rows = m8(first_row, SLICE)
            buf[rows, :] -= 3.0 * pb[k, rows, :]

    def split_block(first, last):
        for load in loads[first:last]:
            load.wait()

        def tile(i, carry):
            value = xf[pl.ds(pl.multiple_of(i * 64, 64), 64), :]
            hi = value.astype(BF16)
            to = lax.div(i, TILE // 64) * (2 * TILE) + lax.rem(i, TILE // 64) * 64
            xs[pl.ds(pl.multiple_of(to, 64), 64), :] = hi
            xs[pl.ds(pl.multiple_of(to + TILE, 64), 64), :] = (value - hi.astype(F32)).astype(BF16)
            return carry

        lax.fori_loop(first * STEP // 64, last * STEP // 64, tile, 0)

    def chain(k):
        steps = []
        state = {}

        along_x = [sems.new_recv() for _ in range(4)]
        to_relay = [sems.new_recv() for _ in range(2)]
        scattered = [sems.new_recv() for _ in range(4)][0]
        arrive = sems.new_recv()
        ring = [None] + [sems.new_recv() for _ in range(3)]
        share = sems.new_recv()
        source_sent, relay_sent, scatter_sent, z_sent, ring_sent, share_sent = [
            sems.new_send() for _ in range(6)
        ]

        def piece(ref, i):
            return ref.at[k, pl.ds(i * QUARTER, QUARTER)]

        def from_source(i):
            return sems.copy(piece(pb, 4 + i), piece(px, i), source_sent, along_x[i], at_x(1))

        def from_source_left(i):
            return sems.copy(piece(pb, 4 + i), piece(px, i), source_sent, along_x[i], at_x(3))

        def to_relay_copy(i):
            return sems.copy(piece(pb, i), piece(pr, i % 2), source_sent, to_relay[i % 2], at_x(1 if i < 2 else 3))

        def relay_copy(i):
            return sems.copy(piece(pr, i % 2), piece(px, i), relay_sent, along_x[i], at_x(1 if i < 2 else 3))

        def scatter_copy(i):
            return sems.copy(piece(px, i), py.at[k, y], scatter_sent, scattered + y, {"row": 2 * i + q})

        def z_copy(src, s):
            return sems.copy(src, pc.at[k, mine(0)], z_sent, arrive, {"col": s * 4 + x})

        def panel_send():
            @pl.when(has_panel)
            def _():
                panel_loads[k].wait()

            @pl.when(source_0)
            def _():
                for i in range(4):
                    from_source(i).start()
                px[k] = pb[k, pl.ds(0, DEPTH)]

            @pl.when(source_1)
            def _():
                for i in (0, 2, 1, 3):
                    to_relay_copy(i).start()
                for i in range(4):
                    from_source_left(i).start()

        def panel_scatter():
            @pl.when(relay_1)
            def _():
                for i in (0, 1):
                    to_relay_copy(i).wait_recv()
                    relay_copy(i).start()

            @pl.when(relay_3)
            def _():
                for i in (2, 3):
                    to_relay_copy(i).wait_recv()
                    relay_copy(i).start()

            @pl.when(holds)
            def _():
                for i in range(4):

                    @pl.when(x != 0)
                    def _(i=i):
                        from_source(i).wait_recv()

                    @pl.when(y != i)
                    def _(i=i):
                        scatter_copy(i).start()

                    if k == 0:
                        split_block(2 * i, 2 * i + 2)

        def panel_along_z():
            @pl.when(holds)
            def _():
                for s in (2, 1, 3, 0):

                    @pl.when(y != s)
                    def _(s=s):
                        sems.got(py.at[k, s], scattered + s)
                        if s:
                            z_copy(py.at[k, s], s).start()
                        else:
                            pc[k, mine(0)] = py[k, 0]

                    @pl.when(y == s)
                    def _(s=s):
                        if s:
                            z_copy(piece(px, s), s).start()
                        else:
                            pc[k, mine(0)] = px[k, pl.ds(0, QUARTER)]

        def mine(d):
            return m8(lax.rem(y + 4 - d, 4) * QUARTER, QUARTER)

        def ring_copy(d):
            return sems.copy(pc.at[k, mine(0)], pc.at[k, mine(0)], ring_sent, ring[d], at_y(d))

        def share_copy(d):
            return sems.copy(pc.at[k, mine(d)], pc.at[k, mine(d)], share_sent, share, partner)

        def panel_ring():
            @pl.when(fetches)
            def _():
                @pl.when(zh != 0)
                def _():
                    sems.got(pc.at[k, mine(0)], arrive)

                for d in (2, 1, 3):
                    ring_copy(d).start()
                share_copy(0).start()

        def panel_share():
            @pl.when(fetches)
            def _():
                for d in (1, 3, 2):
                    ring_copy(d).wait_recv()
                    share_copy(d).start()

            @pl.when(jnp.logical_not(fetches))
            def _():
                sems.got(pc.at[k], share)

        def panel_drain():
            @pl.when(source_0)
            def _():
                sems.sent(px.at[k], source_sent)

            @pl.when(source_1)
            def _():
                sems.sent(pb.at[k], source_sent)

            @pl.when(jnp.logical_or(relay_1, relay_3))
            def _():
                sems.sent(pr.at[k], relay_sent)

            @pl.when(holds)
            def _():
                sems.sent(px.at[k, pl.ds(0, 3 * QUARTER)], scatter_sent)
                sems.sent(px.at[k, pl.ds(0, 3 * QUARTER)], z_sent)

            @pl.when(fetches)
            def _():
                sems.sent(pc.at[k, pl.ds(0, 3 * QUARTER)], ring_sent)
                sems.sent(pc.at[k], share_sent)

        def ring_drain(phase):
            x_rows_sent = part.at[phase, k, pl.ds(0, 3 * SLICE)]
            sems.sent(x_rows_sent, x_sent[phase])
            sems.sent(x_rows_sent, gx_sent[phase])
            sems.sent(part.at[phase, k, pl.ds(0, 6 * SUB)], z_ring_sent[phase])

        x_sent = [sems.new_send() for _ in range(2)]
        gx_sent = [sems.new_send() for _ in range(2)]
        z_ring_sent = [sems.new_send() for _ in range(2)]
        slots = {
            (phase, u, name): sems.new_recv()
            for phase in range(2)
            for u in range(UNITS)
            for name in ("x1", "x2", "z1", "z2", "g1", "g2", "g3", "g4")
        }

        def multiply(phase):
            buf = part.at[phase, k]

            def run(first_row):
                product(buf, k, first_row)
                if phase == 1:
                    minus_panel(buf, k, first_row)

            def step():
                split_rhs((pc if phase == 0 else sc).at[k], k)
                run(x_rows[2])
                for u in range(UNITS):
                    reduce_start(
                        buf, rx1.at[phase, k, u], unit_x[u], US, at_x, x_sent[phase], slots[phase, u, "x1"]
                    )
                run(x_rows[1])
                run(x_rows[3])
                for u in range(UNITS):
                    reduce_own(
                        buf, rx2.at[phase, k, u], unit_x[u], US, at_x, x_sent[phase], slots[phase, u, "x2"]
                    )
                run(x_rows[0])

            return step

        unit_x = [[r + u * US for r in x_rows] for u in range(UNITS)]
        unit_z = [
            [unit_x[u][0] + lax.rem(zh + d, 4) * UZ for d in range(4)] for u in range(UNITS)
        ]

        def unit_steps(phase, u):
            buf = part.at[phase, k]
            out = outs[phase].at[k]
            xr, zr = unit_x[u], unit_z[u]
            xs_, zs_, gs_ = x_sent[phase], z_ring_sent[phase], gx_sent[phase]
            slot = {name: slots[phase, u, name] for name in ("x1", "x2", "z1", "z2", "g1", "g2", "g3", "g4")}

            def x_middle():
                reduce_middle(
                    buf, rx1.at[phase, k, u], rx2.at[phase, k, u], xr, US, at_x, xs_, slot["x1"], slot["x2"]
                )

            def x_end():
                sems.got(rx2.at[phase, k, u], slot["x2"])
                rows = m8(xr[0], US)
                buf[rows] += rx2[phase, k, u, 0] + rx2[phase, k, u, 1]
                reduce_start(buf, rz1.at[phase, k, u], zr, UZ, at_z, zs_, slot["z1"])
                reduce_own(buf, rz2.at[phase, k, u], zr, UZ, at_z, zs_, slot["z2"])

            def z_middle():
                reduce_middle(
                    buf, rz1.at[phase, k, u], rz2.at[phase, k, u], zr, UZ, at_z, zs_, slot["z1"], slot["z2"]
                )

            def z_end():
                sems.got(rz2.at[phase, k, u], slot["z2"])
                rows = m8(zr[0], UZ)
                total = buf[rows] + (rz2[phase, k, u, 0] + rz2[phase, k, u, 1])
                out[rows] = total if phase == 0 else total * -0.5
                gather_start(out, zr, UZ, at_z, zs_, slot["g1"])

            def gz_middle():
                gather_arrived(out, UZ, slot["g1"])
                gather_onward(out, zr, UZ, at_z, zs_, slot["g2"])

            def gx_start():
                sems.got(out.at[pl.ds(0, UZ)], slot["g2"])
                gather_start(out, xr, US, at_x, gs_, slot["g3"])
                if phase == 0:
                    send_slab(u, 0)

            def gx_middle():
                gather_arrived(out, US, slot["g3"])
                if phase == 0:
                    send_slab(u, 1)
                else:
                    gx_onward()

            def gx_onward():
                gather_onward(out, xr, US, at_x, gs_, slot["g4"])

            def gx_end():
                sems.got(out.at[pl.ds(0, US)], slot["g4"])

            return [x_middle, x_end, z_middle, z_end, gz_middle, gx_start, gx_middle, gx_end, gx_onward]

        turn = lax.rem(y - zh + 4, 4)
        root = jnp.logical_and(fetches, turn == 0)
        y1 = jnp.logical_and(fetches, turn == 1)
        y2 = jnp.logical_and(fetches, turn == 2)
        y3 = jnp.logical_and(fetches, turn == 3)
        fwd = {(i, u): sems.new_recv() for i in range(2) for u in range(UNITS)}
        root_sent, onward_sent, across_sent = [sems.new_send() for _ in range(3)]

        def held(i, u):
            return outs[0].at[k, m8(half * DEPTH + i * SLICE + u * US, US)]

        def block(i, u):
            return sc.at[k, pl.ds(i * SLICE + u * US, US)]

        def from_root(i, u, d):
            return sems.copy(held(i, u), block(i, u), root_sent, fwd[i, u], at_y(d))

        def onward(i, u):
            return sems.copy(block(i, u), block(i, u), onward_sent, fwd[i, u], at_y(1 + 2 * i))

        def across(i, u):
            return sems.copy(block(i, u), block(i, u), across_sent, fwd[i, u], partner)

        def send_slab(u, i):
            @pl.when(root)
            def _():
                from_root(i, u, 1).start()
                from_root(i, u, 3).start()
                block(i, u)[...] = held(i, u)[...]
                across(i, u).start()

        def pass_slab(u, i):
            def step():
                for d, here in ((1, y1), (3, y3)):

                    @pl.when(here)
                    def _(d=d):
                        from_root(i, u, d).wait_recv()
                        if d == 1 + 2 * i:
                            onward(i, u).start()
                        across(i, u).start()

            return step

        def end_slab(u, i):
            def step():
                @pl.when(y2)
                def _():
                    onward(i, u).wait_recv()
                    across(i, u).start()

                @pl.when(jnp.logical_not(fetches))
                def _():
                    across(i, u).wait_recv()

            return step

        pieces = [(u, i) for u in range(UNITS) for i in range(2)]

        def slab_drain():
            @pl.when(root)
            def _():
                sems.sent(outs[0].at[k], root_sent)

            @pl.when(jnp.logical_or(y1, y3))
            def _():
                sems.sent(sc.at[k, pl.ds(0, SLICE)], onward_sent)

            @pl.when(fetches)
            def _():
                sems.sent(sc.at[k], across_sent)

            ring_drain(0)
            ring_drain(1)

        panel = [panel_send, panel_scatter, panel_along_z, panel_ring, panel_share]
        named = {("p", i): f for i, f in enumerate(panel)}
        named["m", 0], named["m", 1] = multiply(0), multiply(1)
        for phase in range(2):
            for u in range(UNITS):
                for i, f in enumerate(unit_steps(phase, u)):
                    named["u", phase, u, i] = f
        for u, i in pieces:
            named["s", u, i] = pass_slab(u, i)
            named["e", u, i] = end_slab(u, i)
        return named, [panel_drain, slab_drain], state

    chains = [chain(k) for k in range(CHUNKS)]
    for step in ORDER:
        if step == "split":

            @pl.when(jnp.logical_not(holds))
            def _():
                split_block(0, ROWS // STEP)
        else:
            chains[step[0]][0][step[1:]]()
    for _, ends, state in chains:
        for end in ends:
            end()


def lay_out(square, new, square_out, new_out, sem):
    copies = [
        pltpu.make_async_copy(src.at[k], dst.at[:, pl.ds(k * W, W)], sem.at[i, k])
        for i, (src, dst) in enumerate(((square, square_out), (new, new_out)))
        for k in range(CHUNKS)
    ]
    for copy in copies:
        copy.start()
    for copy in copies:
        copy.wait()


def solution(mesh):
    def body(matrix):
        square, new = pl.pallas_call(
            kernel,
            out_shape=(
                pltpu.VMEM((CHUNKS, ROWS, W), F32),
                pltpu.VMEM((CHUNKS, ROWS, W), F32),
            ),
            in_specs=[pl.BlockSpec(memory_space=pl.ANY)],
            out_specs=(pl.BlockSpec(memory_space=pltpu.VMEM), pl.BlockSpec(memory_space=pltpu.VMEM)),
            scratch_shapes=[
                pltpu.VMEM((ROWS, DEPTH), F32),
                pltpu.VMEM((2 * ROWS, DEPTH), BF16),
                pltpu.VMEM((CHUNKS, ROWS, W), F32),
                pltpu.VMEM((CHUNKS, DEPTH, W), F32),
                pltpu.VMEM((CHUNKS, 2 * QUARTER, W), F32),
                pltpu.VMEM((CHUNKS, 4, QUARTER, W), F32),
                pltpu.VMEM((CHUNKS, DEPTH, W), F32),
                pltpu.VMEM((CHUNKS, DEPTH, W), F32),
                pltpu.VMEM((CHUNKS, DEPTH, 2 * W), BF16),
                pltpu.VMEM((2, CHUNKS, ROWS, W), F32),
                pltpu.VMEM((2, CHUNKS, UNITS, 2, US // 2, W), F32),
                pltpu.VMEM((2, CHUNKS, UNITS, 2, US, W), F32),
                pltpu.VMEM((2, CHUNKS, UNITS, 2, UZ // 2, W), F32),
                pltpu.VMEM((2, CHUNKS, UNITS, 2, UZ, W), F32),
                pltpu.SemaphoreType.DMA((NSEND,)),
                pltpu.SemaphoreType.DMA((NRECV,)),
                pltpu.SemaphoreType.DMA((ROWS // STEP,)),
                pltpu.SemaphoreType.DMA((CHUNKS,)),
            ],
            compiler_params=pltpu.CompilerParams(
                collective_id=0, has_side_effects=True, vmem_limit_bytes=52 * 1024 * 1024
            ),
        )(matrix)
        whole = jax.ShapeDtypeStruct((ROWS, CHUNKS * W), F32)
        anywhere = pl.BlockSpec(memory_space=pl.ANY)
        return pl.pallas_call(
            lay_out,
            out_shape=(whole, whole),
            in_specs=[anywhere, anywhere],
            out_specs=(anywhere, anywhere),
            scratch_shapes=[pltpu.SemaphoreType.DMA((2, CHUNKS))],
            compiler_params=pltpu.CompilerParams(vmem_limit_bytes=1024 * 1024),
        )(square, new)

    return jax.shard_map(
        body,
        mesh=mesh,
        in_specs=(P("row", "col"),),
        out_specs=(P("row", "layer"), P("row", "layer")),
        check_vma=False,
    )
```
